128 devices in a mesh: section: 2 (over x_hi), dp: 4 (over x_lo, core), tensor: 16 (over z, y).
Axes of the slice: x: 4 (x_hi: 2, x_lo: 2; x = x_hi * 2 + x_lo), y: 4, z: 4, core: 2. Of those that a mesh axis runs over, the one named last changes fastest.
Arguments:
- incoming: bfloat16 [2, 3, 1024, 8192], P('section', None, ('dp', 'tensor')), may hold values from -6 to 6
- hidden: bfloat16 [2, 3, 1024, 8192], P('section', None, ('dp', 'tensor')), may hold values from -6 to 6
- expert_out: bfloat16 [2, 3, 1024, 2, 8192], P('section', None, ('dp', 'tensor')), may hold values from -0.59765625 to 0.59765625
- routes: int32 [2, 3, 1024, 2], P('section', None, ('dp', 'tensor')), may hold values from 0 to 15, all different within a row; in each aligned block of 16 rows (0 to 15, 16 to 31, ..., all dimensions but the last counted through in order) at most 4 rows name the same one
- expert_back: bfloat16 [2, 3, 4096, 8192], P('section', None, ('dp', 'tensor')), may hold values from -0.59765625 to 0.59765625
- scan_out: bfloat16 [2, 3, 1024, 8192], P('section', None, 'dp', 'tensor'), may hold values from -6 to 6
- gate_in: bfloat16 [2, 3, 1024, 8192], P('section', None, 'dp', 'tensor'), may hold values from -9 to 9
- w_out: bfloat16 [2, 8192, 8192], P('section', 'tensor'), may hold values from -0.0625 to 0.0625
- w_router: bfloat16 [2, 8192, 16], P('section', 'dp'), may hold values from -0.0625 to 0.0625
- norm_gain: bfloat16 [2, 8192], P('section', 'dp'), may hold values from 0.5 to 1.5
Outputs:
- passed: bfloat16 [2, 3, 1024, 8192], P('section', None, ('dp', 'tensor'))
- scan_grad: bfloat16 [2, 3, 1024, 8192], P('section', None, 'dp', 'tensor')
- gate_grad: bfloat16 [2, 3, 1024, 8192], P('section', None, 'dp', 'tensor')
- expert_grad: bfloat16 [2, 3, 4096, 8192], P('section', None, ('dp', 'tensor'))
- w_out_grad: float32 [2, 8192, 8192], P('section', 'tensor', 'dp')
- router_grad: float32 [2, 8192, 16], P('section', 'dp')
- gain_grad: float32 [2, 8192], P('section', 'dp')
The draws below stay inside these ranges and needn't reach their ends.
Inputs may be any that keep to these rules, and one draw needn't show every extreme that they name: `routes`: each row names 2 different experts. In each aligned block of 16 rows (the rows of one device) no expert is named by more than 4 rows, a bound that some block reaches.
All inputs are finite; a program needn't handle non-finite values.
Results may differ from the reference program's by a relative error of at most 0.025.
Values may be sent and summed in bfloat16 or wider, within the bound.
A program may use at most 192 MiB of HBM per device.

```python
import math
import jax
import jax.numpy as jnp
import numpy as np
from jax import lax

D = 8192
DI = 8192
TOPK = 2
TOK_DEV = 16
MICRO = 3
EXPERTS = 16
CAP = 4
GROUP = 256
TOKENS = 1024
SLOT_ROWS = 4096
N_DP = 4
N_TENSOR = 16


def steps_of(rng, extent, split, low, high):
    def one(dim, blocks):
        heights = jax.random.uniform(jax.random.fold_in(jax.random.fold_in(rng, 6), dim), (blocks,), jnp.float32, low / len(split), high / len(split))
        return jnp.repeat(jnp.exp(heights), extent[dim] // blocks).reshape((-1,) + (1,) * (len(extent) - dim - 1))

    level = one(*split[0])
    for cut in split[1:]:
        level = level * one(*cut)
    return level


def assign_block(stream_key, own, number, rows, count, top, bound, skew):
    ranking = jax.random.permutation(stream_key, count)
    packed, ordinary = portions_of(count, rows * top, bound, skew, True), portions_of(count, rows * top, bound, skew, False)
    places = jnp.arange(count)

    def named(tallies, turn):
        used = int((tallies > 0).sum())
        fixed = max(1, used // 4)
        moved = fixed + (places - fixed + turn * (used - fixed)) % max(1, count - fixed)
        return jnp.zeros((count,), jnp.int32).at[ranking[jnp.where(places < fixed, places, moved)]].set(jnp.asarray(tallies, jnp.int32))

    tallies = jnp.where(number % 4 == 0, named(packed, number // 4), named(ordinary, number - number // 4 - 1))
    mixed = jax.random.permutation(jax.random.fold_in(own, 3), count)
    donor, receiver = mixed[0:count // 2 * 2:2], mixed[1:count // 2 * 2:2]
    slack = jnp.minimum(tallies[donor] - 1, bound - tallies[receiver]) // 2
    slack = jnp.where((donor == ranking[0]) | (receiver == ranking[0]) | (tallies[receiver] == 0), 0, jnp.maximum(slack, 0))
    moved = jax.random.randint(jax.random.fold_in(own, 4), (count // 2,), 0, 1 << 20) % (slack + 1)
    tallies = tallies.at[donor].add(-moved).at[receiver].add(moved)
    members = jnp.searchsorted(jnp.cumsum(tallies), jnp.arange(rows * top), side="right").astype(jnp.int32)
    table = members.reshape(top, rows).T
    table = table[jax.random.permutation(jax.random.fold_in(own, 1), rows)]
    turn = jax.random.randint(jax.random.fold_in(own, 2), (rows, 1), 0, top)
    return jnp.take_along_axis(table, (jnp.arange(top)[None, :] + turn) % top, axis=1)


def portions_of(number_of, total, most, skew, full):
    portions = [(1 << 20) // math.isqrt(grade ** skew) + 1 for grade in range(1, number_of + 1)]
    largest = most if full else min(most, max(-(-total // number_of), total * portions[0] // sum(portions)))
    least = 1 if total - largest >= number_of - 1 else 0
    given, rest = [largest] + [least] * (number_of - 1), total - largest - least * (number_of - 1)
    while rest > 0:
        candidates = [i for i in range(1, number_of) if given[i] < largest] or [i for i in range(1, number_of) if given[i] < most]
        mass, left = sum([portions[i] for i in candidates]), rest
        for i in candidates:
            extra = min(most - given[i], max(1, left * portions[i] // mass), rest)
            given[i] = given[i] + extra
            rest = rest - extra
    return np.array(given)


def scatter_about(key, shape, deviation, reach, shards=(), kind=jnp.bfloat16):
    result = deviation * jax.random.normal(key, shape, jnp.float32)
    if shards:
        result = result * steps_of(key, shape, shards, -0.22, 0.18)
    return jnp.clip(result, -reach, reach).astype(kind)


def setup_inputs(seed: int = 0) -> dict:
    seeds = jax.random.split(jax.random.key(seed), 11)
    incoming = scatter_about(seeds[0], (2, MICRO, TOKENS, D), 1.0, 6.0, ((0, 2), (2, 64)))
    hidden = scatter_about(seeds[1], (2, MICRO, TOKENS, D), 1.0, 6.0, ((0, 2), (2, 64)))
    expert_out = scatter_about(seeds[2], (2, MICRO, TOKENS, TOPK, D), 0.1, 0.59765625, ((0, 2), (2, 64)))
    routes_keys = jax.random.split(jax.random.fold_in(seeds[3], 1), 2 * MICRO * TOKENS // TOK_DEV)
    routes_turns = jax.random.permutation(jax.random.fold_in(seeds[3], 3), 2 * MICRO * TOKENS // TOK_DEV)
    routes = jax.vmap(lambda own, number: assign_block(jax.random.fold_in(seeds[3], 2), own, number, TOK_DEV, EXPERTS, TOPK, CAP, 2))(routes_keys, routes_turns).reshape((2, MICRO, TOKENS, TOPK))
    expert_back = scatter_about(seeds[4], (2, MICRO, SLOT_ROWS, D), 0.1, 0.59765625, ((0, 2), (2, 64)))
    scan_out = scatter_about(seeds[5], (2, MICRO, TOKENS, DI), 1.0, 6.0, ((0, 2), (2, 4), (3, 16)))
    gate_in = scatter_about(seeds[6], (2, MICRO, TOKENS, DI), 1.5, 9.0, ((0, 2), (2, 4), (3, 16)))
    w_out = scatter_about(seeds[7], (2, DI, D), DI ** -0.5, 0.0625, ((0, 2), (1, 16)))
    w_router = scatter_about(seeds[8], (2, D, EXPERTS), D ** -0.5, 0.0625, ((0, 2), (1, 4)))
    norm_gain = jnp.clip(1.0 + 0.1 * jax.random.normal(seeds[9], (2, D), jnp.float32), 0.5, 1.5).astype(jnp.bfloat16)
    return {"incoming": incoming, "hidden": hidden, "expert_out": expert_out, "routes": routes, "expert_back": expert_back, "scan_out": scan_out, "gate_in": gate_in, "w_out": w_out, "w_router": w_router, "norm_gain": norm_gain}


def slot_rows(route_ids):
    blocks = TOKENS // TOK_DEV
    flat_ids = route_ids.reshape(blocks, TOK_DEV * TOPK)
    onehot = (flat_ids[:, :, None] == jnp.arange(EXPERTS, dtype=jnp.int32)[None, None, :]).astype(jnp.int32)
    before = jnp.cumsum(onehot, axis=1, dtype=jnp.int32) - onehot
    slot_index = lax.optimization_barrier(jnp.sum(before * onehot, axis=2, dtype=jnp.int32))
    block_ids = jnp.arange(blocks, dtype=jnp.int32)[:, None]
    data_group = block_ids // N_TENSOR
    position = block_ids % N_TENSOR
    return (((data_group * EXPERTS + flat_ids) * N_TENSOR + position) * CAP + slot_index).reshape(-1)

def moe_backward(upstream, hidden_rows, expert_rows, route_ids, back_rows, router, gain):
    hidden_f = hidden_rows.astype(jnp.float32)
    inv_rms = 1.0 / jnp.sqrt(lax.optimization_barrier(jnp.mean(hidden_f * hidden_f, axis=1, keepdims=True)) + 1e-05)
    gain_f = gain.astype(jnp.float32)
    normed = (hidden_f * inv_rms * gain_f).astype(jnp.bfloat16)
    logits = jnp.dot(normed, router, preferred_element_type=jnp.float32)
    weights = jnp.exp(logits)
    route_probs = weights / lax.optimization_barrier(jnp.sum(weights, axis=1, keepdims=True))
    chosen = (route_ids[:, :, None] == jnp.arange(EXPERTS, dtype=jnp.int32)[None, None, :]).astype(jnp.float32)
    route_prob = lax.optimization_barrier(jnp.sum(chosen * route_probs[:, None, :], axis=2))
    upstream_f = upstream.astype(jnp.float32)
    score_grad = jnp.einsum('td,tkd->tk', upstream_f, expert_rows.astype(jnp.float32))
    prob_grad = lax.optimization_barrier(jnp.sum(chosen * score_grad[:, :, None], axis=1))
    logit_grad = (route_probs * (prob_grad - lax.optimization_barrier(jnp.sum(route_probs * prob_grad, axis=1, keepdims=True)))).astype(jnp.bfloat16)
    row_index = slot_rows(route_ids)
    returned = back_rows[row_index].astype(jnp.float32).reshape(TOKENS, TOPK, D)
    norm_grad = jnp.dot(logit_grad, router.T, preferred_element_type=jnp.float32) + lax.optimization_barrier(jnp.sum(returned, axis=1))
    scaled = norm_grad * gain_f
    hidden_grad = inv_rms * scaled - hidden_f * inv_rms ** 3 * lax.optimization_barrier(jnp.mean(scaled * hidden_f, axis=1, keepdims=True))
    passed = (upstream_f + hidden_grad).astype(jnp.bfloat16)
    sent = (route_prob[:, :, None] * upstream_f[:, None, :]).astype(jnp.bfloat16).reshape(TOKENS * TOPK, D)
    expert_grad = jnp.zeros((SLOT_ROWS, D), jnp.bfloat16).at[row_index].set(sent)
    gain_term = lax.optimization_barrier(jnp.sum(norm_grad * hidden_f * inv_rms, axis=0))
    router_term = lax.dot_general(normed, logit_grad, (((0,), (0,)), ((), ())), preferred_element_type=jnp.float32)
    return (passed, expert_grad, gain_term, router_term)

def mixer_backward(passed, scan_rows, gate_rows, weight):
    scan_f = scan_rows.astype(jnp.float32)
    gate_f = gate_rows.astype(jnp.float32)
    sigmoid_gate = jax.nn.sigmoid(gate_f)
    gated = (scan_f * gate_f * sigmoid_gate).astype(jnp.bfloat16)
    inner_grad = lax.dot_general(passed, weight, (((1,), (1,)), ((), ())), preferred_element_type=jnp.float32)
    scan_grad = (inner_grad * gate_f * sigmoid_gate).astype(jnp.bfloat16)
    gate_grad = (inner_grad * scan_f * sigmoid_gate * (1.0 + gate_f * (1.0 - sigmoid_gate))).astype(jnp.bfloat16)
    return (gated, scan_grad, gate_grad)

def reference(incoming, hidden, expert_out, routes, expert_back, scan_out, gate_in, w_out, w_router, norm_gain):
    passed_all = [[], []]
    expert_all = [[], []]
    scan_all = [[], []]
    gate_all = [[], []]
    weight_all = [None, None]
    router_all = [None, None]
    gain_all = [None, None]
    for section_index in (1, 0):
        gain_total = jnp.zeros((D,), jnp.float32)
        router_total = jnp.zeros((D, EXPERTS), jnp.float32)
        gated_list = []
        for micro_step in range(MICRO):
            if section_index == 1 or micro_step == 0:
                upstream = incoming[section_index, micro_step]
            else:
                upstream = passed_all[1][micro_step - 1]
            passed, expert_grad, gain_term, router_term = moe_backward(upstream, hidden[section_index, micro_step], expert_out[section_index, micro_step], routes[section_index, micro_step], expert_back[section_index, micro_step], w_router[section_index], norm_gain[section_index])
            gain_total = gain_total + gain_term
            router_total = router_total + router_term
            gated, scan_grad, gate_grad = mixer_backward(passed, scan_out[section_index, micro_step], gate_in[section_index, micro_step], w_out[section_index])
            passed_all[section_index].append(passed)
            expert_all[section_index].append(expert_grad)
            scan_all[section_index].append(scan_grad)
            gate_all[section_index].append(gate_grad)
            gated_list.append(gated)
        weight_total = jnp.zeros((DI, D), jnp.float32)
        for data_group in range(N_DP):
            first_row = data_group * GROUP
            partial_sum = jnp.zeros((DI, D), jnp.float32)
            for micro_step in range(MICRO):
                gated_rows = gated_list[micro_step][first_row:first_row + GROUP]
                passed_rows = passed_all[section_index][micro_step][first_row:first_row + GROUP]
                partial_sum = partial_sum + lax.dot_general(gated_rows, passed_rows, (((0,), (0,)), ((), ())), preferred_element_type=jnp.float32)
            weight_total = weight_total + lax.optimization_barrier(partial_sum.astype(jnp.bfloat16)).astype(jnp.float32)
        weight_all[section_index] = weight_total
        router_all[section_index] = router_total
        gain_all[section_index] = gain_total
    passed_out = jnp.stack([jnp.stack(passed_all[0]), jnp.stack(passed_all[1])])
    scan_grad_out = jnp.stack([jnp.stack(scan_all[0]), jnp.stack(scan_all[1])])
    gate_grad_out = jnp.stack([jnp.stack(gate_all[0]), jnp.stack(gate_all[1])])
    expert_grad_out = jnp.stack([jnp.stack(expert_all[0]), jnp.stack(expert_all[1])])
    weight_out = jnp.stack(weight_all)
    router_out = jnp.stack(router_all)
    gain_out = jnp.stack(gain_all)
    return (passed_out, scan_grad_out, gate_grad_out, expert_grad_out, weight_out, router_out, gain_out)
```

```python
import jax
import jax.numpy as jnp
from jax import lax
from jax.experimental import pallas as pl
from jax.experimental.pallas import tpu as pltpu
from jax.sharding import PartitionSpec as P

MESH = pl.DeviceIdType.MESH
CHUNKS = 8
QCOL = 256
CCOL = 1024
HALF = 512


def mixer_kernel(
    passed_ref, scan_ref, gate_ref, w_hbm,
    scan_out, gate_out, wgrad_out,
    G, W, gT, inner, own, outv, msend, mrecv, xsend, xrecv, stage,
    ag_s, ag_r, w_sem, ms_s, ms_r, xs_s, xs_r, out_sem, fin_sem,
):
    d = lax.axis_index("dp")
    tau = lax.axis_index("tensor")
    z = tau // 4
    y = tau % 4
    core = d % 2
    xl = d // 2
    mate = xl * 2 + (1 - core)
    xnbr = (1 - xl) * 2 + core

    def at_y(k):
        return z * 4 + (y + k) % 4

    def at_z(k):
        return ((z + k) % 4) * 4 + y

    barrier = pltpu.get_barrier_semaphore()
    for peer in (at_y(1), at_y(3), at_z(1), at_z(3)):
        pl.semaphore_signal(barrier, inc=1, device_id={"tensor": peer}, device_id_type=MESH)
    for peer in (mate, xnbr):
        pl.semaphore_signal(barrier, inc=1, device_id={"dp": peer}, device_id_type=MESH)

    def w_load(c, carry):
        for q in range(4):
            pltpu.make_async_copy(
                w_hbm.at[:, pl.ds(pl.multiple_of(q * 2048 + c * QCOL, QCOL), QCOL)],
                W.at[c, :, pl.ds(q * QCOL, QCOL)],
                w_sem.at[c],
            ).start()
        return carry

    for c in range(CHUNKS):
        for t in range(3):
            for q in range(4):
                G[c, t, z, pl.ds(pl.multiple_of(16 * y, 16), 16), q * QCOL : (q + 1) * QCOL] = (
                    passed_ref[t, :, q * 2048 + c * QCOL : q * 2048 + (c + 1) * QCOL]
                )
    pl.semaphore_wait(barrier, 6)

    def y16(k):
        return pl.ds(pl.multiple_of(16 * ((y + k) % 4), 16), 16)

    def shard(c, h, k, c0, cw):
        if h == 0:
            return G.at[c, :, z, y16(k), pl.ds(h * HALF + c0, cw)]
        return G.at[c, :, (z + k) % 4, y16(0), pl.ds(h * HALF + c0, cw)]

    def block(c, h, k, c0, cw):
        if h == 0:
            return G.at[c, :, (z + k) % 4, :, pl.ds(h * HALF + c0, cw)]
        return G.at[c, :, :, y16(k), pl.ds(h * HALF + c0, cw)]

    def nbr(h, stage_no, step):
        return at_y(step) if (h == 0) == (stage_no == 0) else at_z(step)

    def region(c, h, kind, k):
        fn = shard if kind < 4 else block
        if kind % 4 < 2:
            return fn(c, h, k, 0, HALF)
        return fn(c, h, k, (kind % 2) * (HALF // 2), HALF // 2)

    def ag_copy(c, h, kind, k):
        ref = region(c, h, kind, k)
        return pltpu.make_async_remote_copy(
            src_ref=ref, dst_ref=ref, send_sem=ag_s.at[c, h, kind], recv_sem=ag_r.at[c, h, kind],
            device_id={"tensor": nbr(h, kind // 4, 1 if kind % 2 == 0 else 3)}, device_id_type=MESH,
        )

    def send(c, h, kind):
        step = 0 if kind % 4 < 2 else (3 if kind % 2 == 0 else 1)
        ag_copy(c, h, kind, step).start()

    def recv(c, h, kind):
        step = (3 if kind % 2 == 0 else 1) if kind % 4 < 2 else 2
        ag_copy(c, h, kind, step).wait_recv()

    def t0(c):
        for h in range(2):
            send(c, h, 0)
            send(c, h, 1)

    def t1(c):
        for h in range(2):
            recv(c, h, 0)
            send(c, h, 2)
            recv(c, h, 1)
            send(c, h, 3)

    def t2(c):
        for h in range(2):
            recv(c, h, 2)
            recv(c, h, 3)
            send(c, h, 4)
            send(c, h, 5)

    def t3(c):
        for h in range(2):
            recv(c, h, 4)
            send(c, h, 6)
            recv(c, h, 5)
            send(c, h, 7)

    def mate_copy(c):
        return pltpu.make_async_remote_copy(
            src_ref=msend.at[c % 2], dst_ref=mrecv.at[c], send_sem=ms_s.at[c], recv_sem=ms_r.at[c],
            device_id={"dp": mate}, device_id_type=MESH,
        )

    def x_copy(c):
        return pltpu.make_async_remote_copy(
            src_ref=xsend.at[c % 2], dst_ref=xrecv.at[c], send_sem=xs_s.at[c], recv_sem=xs_r.at[c],
            device_id={"dp": xnbr}, device_id_type=MESH,
        )

    def out_copy(c):
        return pltpu.make_async_copy(
            outv.at[c], wgrad_out.at[:, pl.ds(pl.multiple_of(c * QCOL, QCOL), QCOL)], out_sem.at[c]
        )

    def t4(c):
        for h in range(2):
            recv(c, h, 6)
            recv(c, h, 7)
        pltpu.make_async_copy(W.at[c], W.at[c], w_sem.at[c]).wait()
        for t in range(3):
            rows = G[c, t].reshape(256, CCOL)
            inner[t] += lax.dot_general(
                rows, W[c], (((1,), (1,)), ((), ())), preferred_element_type=jnp.float32
            )

        @pl.when(c >= 2)
        def _():
            mate_copy(c - 2).wait_send()

        for cq in range(2):
            for xq in range(2):
                q = xq * 2 + cq
                cols = slice(q * QCOL, (q + 1) * QCOL)
                part = jnp.zeros((512, QCOL), jnp.float32)
                for t in range(3):
                    part += jnp.dot(
                        gT[:, t * 256 : (t + 1) * 256],
                        G[c, t, :, :, cols].reshape(256, QCOL),
                        preferred_element_type=jnp.float32,
                    )

                @pl.when(core == cq)
                def _():
                    own[c % 2, xq] = part

                @pl.when(core != cq)
                def _():
                    msend[c % 2, xq] = part.astype(jnp.bfloat16)

        mate_copy(c).start()

    def r1(c):
        mate_copy(c).wait_recv()

        @pl.when(c >= 2)
        def _():
            x_copy(c - 2).wait_send()

        xsend[c % 2] = (own[c % 2, 1 - xl] + mrecv[c, 1 - xl].astype(jnp.float32)).astype(jnp.bfloat16)
        x_copy(c).start()
        outv[c] = own[c % 2, xl] + mrecv[c, xl].astype(jnp.float32)

    def r2(c):
        x_copy(c).wait_recv()
        outv[c] += xrecv[c].astype(jnp.float32)
        out_copy(c).start()

    t0(0)
    lax.fori_loop(0, CHUNKS, w_load, 0)
    for t in range(3):
        gate_f = gate_ref[t].astype(jnp.float32)
        gated = scan_ref[t].astype(jnp.float32) * gate_f * jax.nn.sigmoid(gate_f)
        gT[:, t * 256 : (t + 1) * 256] = gated.T.astype(jnp.bfloat16)
    inner[...] = jnp.zeros_like(inner)

    def step(s, carry):
        for lag, fn in ((0, t0), (3, t3), (2, t2), (1, t1), (5, r1), (6, r2), (4, t4)):
            low = lag + (1 if fn is t0 else 0)

            @pl.when((s >= low) & (s < CHUNKS + lag))
            def _():
                fn(s - lag)

        return carry

    lax.fori_loop(0, CHUNKS + 7, step, 0)

    for t in range(3):
        gate_f = gate_ref[t].astype(jnp.float32)
        sig = jax.nn.sigmoid(gate_f)
        rows = inner[t]
        stage[0, t] = (rows * gate_f * sig).astype(jnp.bfloat16)
        stage[1, t] = (
            rows * scan_ref[t].astype(jnp.float32) * sig * (1.0 + gate_f * (1.0 - sig))
        ).astype(jnp.bfloat16)
    fin = [
        pltpu.make_async_copy(stage.at[0], scan_out, fin_sem.at[0]),
        pltpu.make_async_copy(stage.at[1], gate_out, fin_sem.at[1]),
    ]
    for cp in fin:
        cp.start()

    def drain(c, carry):
        for h in range(2):
            for kind in range(8):
                ag_copy(c, h, kind, 0 if kind % 4 < 2 else (3 if kind % 2 == 0 else 1)).wait_send()
        out_copy(c).wait()
        return carry

    lax.fori_loop(0, CHUNKS, drain, 0)
    for c in (CHUNKS - 2, CHUNKS - 1):
        mate_copy(c).wait_send()
        x_copy(c).wait_send()
    for cp in fin:
        cp.wait()


def mixer(passed, scan, gate, weight):
    bf16, f32 = jnp.bfloat16, jnp.float32
    vmem = pl.BlockSpec(memory_space=pltpu.VMEM)
    hbm = pl.BlockSpec(memory_space=pl.ANY)
    return pl.pallas_call(
        mixer_kernel,
        out_shape=(
            jax.ShapeDtypeStruct((3, 256, 512), bf16),
            jax.ShapeDtypeStruct((3, 256, 512), bf16),
            jax.ShapeDtypeStruct((512, 2048), f32),
        ),
        in_specs=[vmem, vmem, vmem, hbm],
        out_specs=(hbm, hbm, hbm),
        scratch_shapes=[
            pltpu.VMEM((CHUNKS, 3, 4, 64, CCOL), bf16),
            pltpu.VMEM((CHUNKS, 512, CCOL), bf16),
            pltpu.VMEM((512, 768), bf16),
            pltpu.VMEM((3, 256, 512), f32),
            pltpu.VMEM((2, 2, 512, QCOL), f32),
            pltpu.VMEM((CHUNKS, 512, QCOL), f32),
            pltpu.VMEM((2, 2, 512, QCOL), bf16),
            pltpu.VMEM((CHUNKS, 2, 512, QCOL), bf16),
            pltpu.VMEM((2, 512, QCOL), bf16),
            pltpu.VMEM((CHUNKS, 512, QCOL), bf16),
            pltpu.VMEM((2, 3, 256, 512), bf16),
            pltpu.SemaphoreType.DMA((CHUNKS, 2, 8)),
            pltpu.SemaphoreType.DMA((CHUNKS, 2, 8)),
            pltpu.SemaphoreType.DMA((CHUNKS,)),
            pltpu.SemaphoreType.DMA((CHUNKS,)),
            pltpu.SemaphoreType.DMA((CHUNKS,)),
            pltpu.SemaphoreType.DMA((CHUNKS,)),
            pltpu.SemaphoreType.DMA((CHUNKS,)),
            pltpu.SemaphoreType.DMA((CHUNKS,)),
            pltpu.SemaphoreType.DMA((2,)),
        ],
        compiler_params=pltpu.CompilerParams(
            collective_id=0, has_side_effects=True, vmem_limit_bytes=60 * 1024 * 1024
        ),
        cost_estimate=pl.CostEstimate(flops=13_000_000_000, bytes_accessed=30_000_000, transcendentals=0),
    )(passed, scan, gate, weight)


def passed_along(shard, axis, by):
    length = lax.axis_size(axis)
    pairs = [(i, i + by) for i in range(length) if 0 <= i + by < length]
    return lax.ppermute(shard, axis, pairs)


def slot_rows(expert_ids, experts, capacity):
    flat_ids = expert_ids.reshape(-1)
    onehot = (flat_ids[:, None] == jnp.arange(experts, dtype=jnp.int32)[None, :]).astype(jnp.int32)
    before = jnp.cumsum(onehot, axis=0, dtype=jnp.int32) - onehot
    slot_index = jnp.sum(before * onehot, axis=1, dtype=jnp.int32)
    return flat_ids * capacity + slot_index


def on_device(
    incoming, hidden, expert_out, routes, expert_back, scan_out, gate_in, w_out, w_router, norm_gain
):
    micro_count = incoming.shape[1]
    tok_rows = incoming.shape[2]
    model_width = incoming.shape[3]
    top_count = routes.shape[3]
    experts = w_router.shape[2]
    tensor_size = lax.axis_size("tensor")
    capacity = expert_back.shape[2] // tensor_size
    inner_width = scan_out.shape[3]
    weight_rows = w_out[0]
    section_id = lax.axis_index("section")
    router_full, gain_full = (
        lax.all_gather(w_router[0], "dp", axis=0, tiled=True),
        lax.all_gather(norm_gain[0], "dp", axis=0, tiled=True),
    )
    gain_f = gain_full.astype(jnp.float32)
    expert_range = jnp.arange(experts, dtype=jnp.int32)
    router_acc = jnp.zeros((model_width, experts), jnp.float32)
    gain_acc = jnp.zeros((model_width,), jnp.float32)
    passed_list = []
    expert_list = []
    received = incoming[0, 0]
    for micro_step in range(micro_count):
        upstream = incoming[0, micro_step]
        if micro_step > 0:
            upstream = jnp.where(section_id == 1, upstream, received)
        returned = lax.all_to_all(
            expert_back[0, micro_step], "tensor", split_axis=0, concat_axis=0, tiled=True
        )
        hidden_f = hidden[0, micro_step].astype(jnp.float32)
        inv_rms = 1.0 / jnp.sqrt(jnp.mean(hidden_f * hidden_f, axis=1, keepdims=True) + 1e-05)
        normed = (hidden_f * inv_rms * gain_f).astype(jnp.bfloat16)
        logits = jnp.dot(normed, router_full, preferred_element_type=jnp.float32)
        weights = jnp.exp(logits)
        route_probs = weights / jnp.sum(weights, axis=1, keepdims=True)
        expert_ids = routes[0, micro_step]
        chosen = (expert_ids[:, :, None] == expert_range[None, None, :]).astype(jnp.float32)
        route_prob = jnp.sum(chosen * route_probs[:, None, :], axis=2)
        score_grad = jnp.einsum(
            "td,tkd->tk", upstream, expert_out[0, micro_step], preferred_element_type=jnp.float32
        )
        prob_grad = jnp.sum(chosen * score_grad[:, :, None], axis=1)
        logit_grad = (
            route_probs * (prob_grad - jnp.sum(route_probs * prob_grad, axis=1, keepdims=True))
        ).astype(jnp.bfloat16)
        row_index = slot_rows(expert_ids, experts, capacity)
        back_rows = (
            returned[row_index].astype(jnp.float32).reshape(tok_rows, top_count, model_width)
        )
        router_back = lax.dot_general(
            logit_grad, router_full, (((1,), (1,)), ((), ())), preferred_element_type=jnp.float32
        )
        norm_grad = router_back + jnp.sum(back_rows, axis=1)
        scaled = norm_grad * gain_f
        hidden_grad = inv_rms * scaled - hidden_f * inv_rms**3 * jnp.mean(
            scaled * hidden_f, axis=1, keepdims=True
        )
        upstream_f = upstream.astype(jnp.float32)
        passed = (upstream_f + hidden_grad).astype(jnp.bfloat16)
        if micro_step + 1 < micro_count:
            received = passed_along(passed, "section", -1)
        gain_acc = gain_acc + jnp.sum(norm_grad * hidden_f * inv_rms, axis=0)
        router_acc = router_acc + lax.dot_general(
            normed, logit_grad, (((0,), (0,)), ((), ())), preferred_element_type=jnp.float32
        )
        sent = (
            (route_prob[:, :, None] * upstream_f[:, None, :])
            .astype(jnp.bfloat16)
            .reshape(tok_rows * top_count, model_width)
        )
        send_buffer = (
            jnp.zeros((experts * capacity, model_width), jnp.bfloat16).at[row_index].set(sent)
        )
        dispatched = lax.all_to_all(send_buffer, "tensor", split_axis=0, concat_axis=0, tiled=True)
        passed_list.append(passed)
        expert_list.append(dispatched)
    passed_all = jnp.stack(passed_list)
    scan_grad, gate_grad, weight_grad = mixer(passed_all, scan_out[0], gate_in[0], weight_rows)
    summed = (
        lax.psum(router_acc.astype(jnp.bfloat16), "tensor").astype(jnp.float32),
        lax.psum(gain_acc.astype(jnp.bfloat16), "tensor").astype(jnp.float32),
    )
    router_part, gain_part = (
        lax.psum_scatter(
            summed[0].astype(jnp.bfloat16), "dp", scatter_dimension=0, tiled=True
        ).astype(jnp.float32),
        lax.psum_scatter(
            summed[1].astype(jnp.bfloat16), "dp", scatter_dimension=0, tiled=True
        ).astype(jnp.float32),
    )
    return (
        passed_all[None],
        scan_grad[None],
        gate_grad[None],
        jnp.stack(expert_list)[None],
        weight_grad[None],
        router_part[None],
        gain_part[None],
    )


def solution(mesh):
    placed = (
        P("section", None, ("dp", "tensor"), None),
        P("section", None, ("dp", "tensor"), None),
        P("section", None, ("dp", "tensor"), None, None),
        P("section", None, ("dp", "tensor"), None),
        P("section", None, ("dp", "tensor"), None),
        P("section", None, "dp", "tensor"),
        P("section", None, "dp", "tensor"),
        P("section", "tensor", None),
        P("section", "dp", None),
        P("section", "dp"),
    )
    return jax.shard_map(
        on_device,
        mesh=mesh,
        in_specs=placed,
        out_specs=(
            P("section", None, ("dp", "tensor"), None),
            P("section", None, "dp", "tensor"),
            P("section", None, "dp", "tensor"),
            P("section", None, ("dp", "tensor"), None),
            P("section", "tensor", "dp"),
            P("section", "dp", None),
            P("section", "dp"),
        ),
        check_vma=False,
    )
```

```python
import jax
import jax.numpy as jnp
from jax import lax
from jax.experimental import pallas as pl
from jax.experimental.pallas import tpu as pltpu
from jax.sharding import PartitionSpec as P

MESH = pl.DeviceIdType.MESH
MICRO = 3
TOK = 16
WIDTH = 8192
EXPERTS = 16
SLOTS = 64
QB = 2048
CHUNKS = 8
QCOL = 256
CCOL = 1024
HALF = 512
OUTV = 4
WBUF = 3
F32 = jnp.float32
BF16 = jnp.bfloat16


def dot(a, b, dims):
    return lax.dot_general(a, b, ((dims[0], dims[1]), ((), ())), preferred_element_type=F32)


def iota(shape, dim):
    return lax.broadcasted_iota(jnp.int32, shape, dim)


def layer_kernel(
    inc_hbm, hid_ref, eo_ref, routes_ref, routes_t_ref, back_hbm, scan_ref, gate_ref, w_hbm, rg_ref,
    passed_out, scan_out, gate_out, exp_out, wgrad_out, rg_out,
    G, W, gT, inner, own, outv, msend, mrecv, xsend, xrecv, stage,
    UP, PO, NR, RG, NG, RGA, RA, RB, RBR, RC, BR1, BR2, BP, DS, DR, DP,
    probs_s, prob64_s, sel_s, selb_s, inv_s,
    ag_s, ag_r, w_sem, ms_s, ms_r, xs_s, xs_r, out_sem, fin_sem, po_sem,
    b1_s, b1_r, b2_s, b2_r, d1_s, d1_r, d2_s, d2_r, rg_s, rg_r, up_l, up_s, up_r,
    ra_s, ra_r, rb_s, rb_r, rc_s, rc_r,
):
    sec = lax.axis_index("section")
    d = lax.axis_index("dp")
    tau = lax.axis_index("tensor")
    z = tau // 4
    y = tau % 4
    core = d % 2
    xl = d // 2
    mate = xl * 2 + (1 - core)
    xnbr = (1 - xl) * 2 + core

    def at_y(k):
        return z * 4 + (y + k) % 4

    def at_z(k):
        return ((z + k) % 4) * 4 + y

    def al(v, m):
        return pl.multiple_of(v, m)

    def rows16(v):
        return pl.ds(al(16 * v, 16), 16)

    def remote(src, dst, ssem, rsem, peer):
        return pltpu.make_async_remote_copy(
            src_ref=src, dst_ref=dst, send_sem=ssem, recv_sem=rsem, device_id=peer, device_id_type=MESH
        )

    barrier = pltpu.get_barrier_semaphore()

    def greet(k, carry):
        pl.semaphore_signal(barrier, inc=1, device_id={"tensor": (tau + k) % 16}, device_id_type=MESH)
        return carry

    lax.fori_loop(1, 16, greet, 0)
    for k in range(1, 4):
        pl.semaphore_signal(barrier, inc=1, device_id={"dp": (d + k) % 4}, device_id_type=MESH)
    pl.semaphore_signal(barrier, inc=1, device_id={"section": 1 - sec}, device_id_type=MESH)

    def up_local(t):
        return pltpu.make_async_copy(inc_hbm.at[t], UP.at[t], up_l.at[t])

    up_local(0).start()

    @pl.when(sec == 1)
    def _():
        up_local(1).start()
        up_local(2).start()

    def w_start(c):
        for q in range(4):
            pltpu.make_async_copy(
                w_hbm.at[:, pl.ds(al(q * QB + c * QCOL, QCOL), QCOL)],
                W.at[c % WBUF, :, pl.ds(q * QCOL, QCOL)],
                w_sem.at[c % WBUF],
            ).start()

    def b1_copy(t, k, recv):
        if recv:
            ref = BR1.at[t, rows16((z + 4 - k) % 4)]
            return remote(ref, ref, b1_s.at[t, k], b1_r.at[t, k], {"tensor": at_z(k)})
        return remote(
            back_hbm.at[t, rows16((z + k) % 4)], BR1.at[t, rows16(z)],
            b1_s.at[t, k], b1_r.at[t, k], {"tensor": at_z(k)},
        )

    def b1_local(t):
        return pltpu.make_async_copy(back_hbm.at[t, rows16(z)], BR1.at[t, rows16(z)], b1_r.at[t, 0])

    def b2_copy(t, k, recv):
        if recv:
            ref = BR2.at[t, rows16((y + 4 - k) % 4)]
            return remote(ref, ref, b2_s.at[t, k], b2_r.at[t, k], {"tensor": at_y(k)})
        return remote(
            BP.at[t % 2, rows16((y + k) % 4)], BR2.at[t, rows16(y)],
            b2_s.at[t, k], b2_r.at[t, k], {"tensor": at_y(k)},
        )

    def d1_copy(t, k, recv):
        if recv:
            ref = DR.at[t, rows16((y + 4 - k) % 4)]
            return remote(ref, ref, d1_s.at[t, k], d1_r.at[t, k], {"tensor": at_y(k)})
        return remote(
            DS.at[t % 2, rows16((y + k) % 4)], DR.at[t, rows16(y)],
            d1_s.at[t, k], d1_r.at[t, k], {"tensor": at_y(k)},
        )

    def d2_copy(t, k, recv):
        if recv:
            ref = exp_out.at[t, rows16((z + 4 - k) % 4)]
            return remote(ref, ref, d2_s.at[t, k], d2_r.at[t, k], {"tensor": at_z(k)})
        return remote(
            DP.at[t % 2, rows16((z + k) % 4)], exp_out.at[t, rows16(z)],
            d2_s.at[t, k], d2_r.at[t, k], {"tensor": at_z(k)},
        )

    def d2_local(t):
        return pltpu.make_async_copy(DP.at[t % 2, rows16(z)], exp_out.at[t, rows16(z)], d2_r.at[t, 0])

    def rg_copy(k, recv):
        ref = RG.at[(d + 4 - k) % 4] if recv else RG.at[d]
        return remote(ref if recv else rg_ref, ref, rg_s.at[k], rg_r.at[k], {"dp": (d + k) % 4})

    pl.semaphore_wait(barrier, 19)

    for k in range(1, 4):
        rg_copy(k, False).start()
    for t in range(MICRO):
        for k in (2, 1, 3):
            b1_copy(t, k, False).start()
        b1_local(t).start()
    for c in range(WBUF):
        w_start(c)
    RG[d] = rg_ref[...]

    slot_r = iota((SLOTS, TOK), 0)
    slot_e = ((slot_r >> 2) & 3) * 4 + (slot_r >> 4)
    slot_c = slot_r & 3
    slot_rb = iota((TOK, SLOTS), 1)
    slot_eb = ((slot_rb >> 2) & 3) * 4 + (slot_rb >> 4)
    slot_cb = slot_rb & 3
    perm_in = iota((SLOTS, SLOTS), 1)
    perm_out = iota((SLOTS, SLOTS), 0)
    perm = (perm_in == ((perm_out >> 2) & 3) * 16 + (perm_out >> 4) * 4 + (perm_out & 3)).astype(F32).astype(BF16)
    upper = (iota((TOK, TOK), 0) < iota((TOK, TOK), 1)).astype(F32).astype(BF16)
    lower = (iota((TOK, TOK), 0) > iota((TOK, TOK), 1)).astype(F32).astype(BF16)

    RGA[...] = jnp.zeros_like(RGA)
    for k in range(1, 4):
        rg_copy(k, True).wait_recv()

    def gain_of(q):
        return RG[q, EXPERTS : EXPERTS + 1, :].astype(F32)

    def hid_of(t, q):
        return hid_ref[t, :, q * QB : (q + 1) * QB].astype(F32)

    def prepare(t, carry):
        total = jnp.zeros((TOK, 1), F32)
        for q in range(4):
            h = hid_of(t, q)
            total += jnp.sum(h * h, axis=1, keepdims=True)
        inv = 1.0 / jnp.sqrt(total / WIDTH + 1e-05)
        inv_s[t] = inv
        logits = jnp.zeros((TOK, EXPERTS), F32)
        logits_t = jnp.zeros((EXPERTS, TOK), F32)
        for q in range(4):
            normed = (hid_of(t, q) * inv * gain_of(q)).astype(BF16)
            NR[t, :, q * QB : (q + 1) * QB] = normed
            router = RG[q, 0:EXPERTS, :]
            logits += dot(normed, router, ((1,), (1,)))
            logits_t += dot(router, normed, ((1,), (1,)))
        weights = jnp.exp(logits)
        probs_s[t] = weights / jnp.sum(weights, axis=1, keepdims=True)
        weights_t = jnp.exp(logits_t)
        probs_t = weights_t / jnp.sum(weights_t, axis=0, keepdims=True)
        spread = jnp.zeros((SLOTS, TOK), F32)
        for e in range(EXPERTS):
            spread = jnp.where(slot_e == e, probs_t[e : e + 1, :], spread)
        rt0 = routes_t_ref[t, 0:1, :]
        rt1 = routes_t_ref[t, 1:2, :]
        named = ((rt0 == slot_e) | (rt1 == slot_e)).astype(F32)
        before = dot(named.astype(BF16), upper, ((1,), (0,)))
        sel = jnp.where(before == slot_c.astype(F32), named, 0.0)
        sel_s[t] = sel.astype(BF16)
        prob64_s[t] = jnp.sum(sel * spread, axis=1, keepdims=True)
        r0 = routes_ref[t, :, 0:1]
        r1 = routes_ref[t, :, 1:2]
        named_b = ((r0 == slot_eb) | (r1 == slot_eb)).astype(F32)
        before_b = dot(lower, named_b.astype(BF16), ((1,), (0,)))
        selb_s[t] = jnp.where(before_b == slot_cb.astype(F32), named_b, 0.0).astype(BF16)
        return carry

    lax.fori_loop(0, MICRO, prepare, 0)

    def dispatch(t):
        @pl.when(t >= 2)
        def _():
            for k in range(1, 4):
                d1_copy(t - 2, k, False).wait_send()

        prob = prob64_s[t]
        sel = sel_s[t]
        for q in range(4):
            cols = slice(q * QB, (q + 1) * QB)
            DS[t % 2, :, cols] = (dot(sel, UP[t, :, cols], ((1,), (0,))) * prob).astype(BF16)
        for k in (2, 1, 3):
            d1_copy(t, k, False).start()
        DR[t, rows16(y), :] = DS[t % 2, rows16(y), :]

    def dispatch_relay(t):
        for k in range(1, 4):
            d1_copy(t, k, True).wait_recv()

        @pl.when(t >= 2)
        def _():
            for k in range(1, 4):
                d2_copy(t - 2, k, False).wait_send()
            d2_local(t - 2).wait()

        for q in range(4):
            cols = slice(q * QB, (q + 1) * QB)
            DP[t % 2, :, cols] = dot(perm, DR[t, :, cols], ((1,), (0,))).astype(BF16)
        for k in (2, 1, 3):
            d2_copy(t, k, False).start()
        d2_local(t).start()

    def back_relay(t):
        for k in range(1, 4):
            b1_copy(t, k, True).wait_recv()
        b1_local(t).wait()

        @pl.when(t >= 2)
        def _():
            for k in range(1, 4):
                b2_copy(t - 2, k, False).wait_send()

        for q in range(4):
            cols = slice(q * QB, (q + 1) * QB)
            BP[t % 2, :, cols] = dot(perm, BR1[t, :, cols], ((1,), (0,))).astype(BF16)
        for k in (2, 1, 3):
            b2_copy(t, k, False).start()
        BR2[t, rows16(y), :] = BP[t % 2, rows16(y), :]

    def up_copy(t):
        return remote(PO.at[t - 1], UP.at[t], up_s.at[t], up_r.at[t], {"section": 1 - sec})

    def po_copy(t):
        return pltpu.make_async_copy(PO.at[t], passed_out.at[t], po_sem.at[t])

    def upstream_ready(t):
        @pl.when((sec == 1) | (t == 0))
        def _():
            up_local(t).wait()

        @pl.when((sec == 0) & (t > 0))
        def _():
            up_copy(t).wait_recv()

    def combine(t):
        for k in range(1, 4):
            b2_copy(t, k, True).wait_recv()
        scores = jnp.zeros((TOK, 2 * TOK), F32)
        for q in range(4):
            cols = slice(q * QB, (q + 1) * QB)
            scores += dot(UP[t, :, cols], eo_ref[t, :, cols], ((1,), (1,)))
        row_i = iota((TOK, 2 * TOK), 0)
        col_i = iota((TOK, 2 * TOK), 1)
        s0 = jnp.sum(jnp.where(col_i == 2 * row_i, scores, 0.0), axis=1, keepdims=True)
        s1 = jnp.sum(jnp.where(col_i == 2 * row_i + 1, scores, 0.0), axis=1, keepdims=True)
        expert_i = iota((TOK, EXPERTS), 1)
        prob_grad = jnp.where(routes_ref[t, :, 0:1] == expert_i, s0, 0.0) + jnp.where(
            routes_ref[t, :, 1:2] == expert_i, s1, 0.0
        )
        probs = probs_s[t]
        logit_grad = (
            probs * (prob_grad - jnp.sum(probs * prob_grad, axis=1, keepdims=True))
        ).astype(BF16)
        inv = inv_s[t]
        selb = selb_s[t]
        mean = jnp.zeros((TOK, 1), F32)
        for q in range(4):
            cols = slice(q * QB, (q + 1) * QB)
            norm_grad = dot(logit_grad, RG[q, 0:EXPERTS, :], ((1,), (0,))) + dot(
                selb, BR2[t, :, cols], ((1,), (0,))
            )
            NG[:, cols] = norm_grad
            h = hid_of(t, q)
            mean += jnp.sum(norm_grad * gain_of(q) * h, axis=1, keepdims=True)
            RGA[q, EXPERTS : EXPERTS + 1, :] += jnp.sum(norm_grad * h * inv, axis=0, keepdims=True)
            RGA[q, 0:EXPERTS, :] += dot(logit_grad, NR[t, :, cols], ((0,), (0,)))
        mean = mean / WIDTH
        for q in range(4):
            cols = slice(q * QB, (q + 1) * QB)
            hidden_grad = inv * (NG[:, cols] * gain_of(q)) - hid_of(t, q) * (inv * inv * inv) * mean
            passed = (UP[t, :, cols].astype(F32) + hidden_grad).astype(BF16)
            PO[t, :, cols] = passed
            for c in range(CHUNKS):
                G[c, t, z, rows16(y), q * QCOL : (q + 1) * QCOL] = passed[:, c * QCOL : (c + 1) * QCOL]

        @pl.when((sec == 1) & (t < MICRO - 1))
        def _():
            up_copy(t + 1).start()

        po_copy(t).start()

    upstream_ready(0)

    def front(s, carry):
        @pl.when(s == 0)
        def _():
            dispatch(0)

        @pl.when(s < MICRO)
        def _():
            back_relay(s)

        @pl.when(s >= 1)
        def _():
            @pl.when(s >= 2)
            def _():
                upstream_ready(s - 1)

            combine(s - 1)

        @pl.when(s >= 2)
        def _():
            dispatch(s - 1)

        @pl.when((s == 1) | (s == 3))
        def _():
            dispatch_relay((s - 1) // 2)

        return carry

    for t in range(MICRO):
        gate_f = gate_ref[t].astype(F32)
        gated = scan_ref[t].astype(F32) * gate_f * jax.nn.sigmoid(gate_f)
        gT[:, t * 256 : (t + 1) * 256] = gated.T.astype(BF16)
    inner[...] = jnp.zeros_like(inner)
    lax.fori_loop(0, MICRO + 1, front, 0)

    def shard(c, h, k, c0, cw):
        cols = pl.ds(h * HALF + c0, cw)
        if h == 0:
            return G.at[c, :, z, rows16((y + k) % 4), cols]
        return G.at[c, :, (z + k) % 4, rows16(y), cols]

    def block(c, h, k, c0, cw):
        cols = pl.ds(h * HALF + c0, cw)
        if h == 0:
            return G.at[c, :, (z + k) % 4, :, cols]
        return G.at[c, :, :, rows16((y + k) % 4), cols]

    def ag_copy(c, h, kind, k):
        fn = shard if kind < 4 else block
        if kind % 4 < 2:
            ref = fn(c, h, k, 0, HALF)
        else:
            ref = fn(c, h, k, (kind % 2) * (HALF // 2), HALF // 2)
        step = 1 if kind % 2 == 0 else 3
        peer = at_y(step) if (h == 0) == (kind < 4) else at_z(step)
        return remote(ref, ref, ag_s.at[c, h, kind], ag_r.at[c, h, kind], {"tensor": peer})

    def send_step(kind):
        return 0 if kind % 4 < 2 else (3 if kind % 2 == 0 else 1)

    def send(c, h, kind):
        ag_copy(c, h, kind, send_step(kind)).start()

    def recv(c, h, kind):
        step = (3 if kind % 2 == 0 else 1) if kind % 4 < 2 else 2
        ag_copy(c, h, kind, step).wait_recv()

    def t0(c):
        for h in range(2):
            send(c, h, 0)
            send(c, h, 1)

    def t1(c):
        for h in range(2):
            recv(c, h, 0)
            send(c, h, 2)
            recv(c, h, 1)
            send(c, h, 3)

    def t2(c):
        for h in range(2):
            recv(c, h, 2)
            recv(c, h, 3)
            send(c, h, 4)
            send(c, h, 5)

    def t3(c):
        for h in range(2):
            recv(c, h, 4)
            send(c, h, 6)
            recv(c, h, 5)
            send(c, h, 7)

    def mate_copy(c):
        return remote(msend.at[c % 2], mrecv.at[c], ms_s.at[c], ms_r.at[c], {"dp": mate})

    def x_copy(c):
        return remote(xsend.at[c % 2], xrecv.at[c], xs_s.at[c], xs_r.at[c], {"dp": xnbr})

    def out_copy(c):
        return pltpu.make_async_copy(
            outv.at[c % OUTV], wgrad_out.at[:, pl.ds(al(c * QCOL, QCOL), QCOL)], out_sem.at[c]
        )

    def t4(c):
        for h in range(2):
            recv(c, h, 6)
            recv(c, h, 7)
        w_now = W.at[c % WBUF]
        pltpu.make_async_copy(w_now, w_now, w_sem.at[c % WBUF]).wait()
        for t in range(MICRO):
            inner[t] += dot(G[c, t].reshape(256, CCOL), W[c % WBUF], ((1,), (1,)))

        @pl.when(c + WBUF < CHUNKS)
        def _():
            w_start(c + WBUF)

        @pl.when(c >= 2)
        def _():
            mate_copy(c - 2).wait_send()

        for cq in range(2):
            for xq in range(2):
                q = xq * 2 + cq
                cols = slice(q * QCOL, (q + 1) * QCOL)
                part = jnp.zeros((512, QCOL), F32)
                for t in range(MICRO):
                    part += dot(
                        gT[:, t * 256 : (t + 1) * 256], G[c, t, :, :, cols].reshape(256, QCOL), ((1,), (0,))
                    )

                @pl.when(core == cq)
                def _():
                    own[c % 2, xq] = part

                @pl.when(core != cq)
                def _():
                    msend[c % 2, xq] = part.astype(BF16)

        mate_copy(c).start()

    def r1(c):
        mate_copy(c).wait_recv()

        @pl.when(c >= 2)
        def _():
            x_copy(c - 2).wait_send()

        @pl.when(c >= OUTV)
        def _():
            out_copy(c - OUTV).wait()

        xsend[c % 2] = (own[c % 2, 1 - xl] + mrecv[c, 1 - xl].astype(F32)).astype(BF16)
        x_copy(c).start()
        outv[c % OUTV] = own[c % 2, xl] + mrecv[c, xl].astype(F32)

    def r2(c):
        x_copy(c).wait_recv()
        outv[c % OUTV] += xrecv[c].astype(F32)
        out_copy(c).start()

    def ra_copy(k, recv):
        dst = RA.at[(d + 4 - k) % 4] if recv else RA.at[d]
        src = dst if recv else RGA.at[(d + k) % 4]
        return remote(src, dst, ra_s.at[k], ra_r.at[k], {"dp": (d + k) % 4})

    def piece(v):
        return pl.ds(al(128 * v, 128), 128)

    def rb_copy(k, recv):
        dst = RBR.at[(tau + 16 - k) % 16] if recv else RBR.at[tau]
        src = dst if recv else RB.at[:, piece((tau + k) % 16)]
        return remote(src, dst, rb_s.at[k], rb_r.at[k], {"tensor": (tau + k) % 16})

    def rc_copy(k, recv):
        dst = RC.at[:, piece((tau + 16 - k) % 16)] if recv else RC.at[:, piece(tau)]
        return remote(dst, dst, rc_s.at[k], rc_r.at[k], {"tensor": (tau + k) % 16})

    def each_peer(fn):
        def go(k, carry):
            fn(k)
            return carry

        lax.fori_loop(1, 16, go, 0)

    def grads_a():
        for k in range(1, 4):
            ra_copy(k, False).start()
        RA[d] = RGA[d]

    def grads_b():
        for k in range(1, 4):
            ra_copy(k, True).wait_recv()
        RB[...] = RA[0] + RA[1] + RA[2] + RA[3]
        each_peer(lambda k: rb_copy(k, False).start())
        RBR[tau] = RB[:, piece(tau)]

    def grads_c():
        each_peer(lambda k: rb_copy(k, True).wait_recv())
        total = RBR[0]
        for k in range(1, 16):
            total += RBR[k]
        RC[:, piece(tau)] = total
        each_peer(lambda k: rc_copy(k, False).start())

    rg_fin = pltpu.make_async_copy(RC, rg_out, fin_sem.at[2])

    def grads_d():
        each_peer(lambda k: rc_copy(k, True).wait_recv())
        rg_fin.start()

    t0(0)
    grads_a()

    def step(s, carry):
        for lag, fn in ((0, t0), (3, t3), (2, t2), (1, t1), (5, r1), (6, r2), (4, t4)):
            low = lag + (1 if fn is t0 else 0)

            @pl.when((s >= low) & (s < CHUNKS + lag))
            def _():
                fn(s - lag)

        @pl.when(s == 1)
        def _():
            dispatch_relay(2)

        for when, fn in ((2, grads_b), (5, grads_c), (8, grads_d)):

            @pl.when(s == when)
            def _():
                fn()

        return carry

    lax.fori_loop(0, CHUNKS + 7, step, 0)

    for t in range(MICRO):
        gate_f = gate_ref[t].astype(F32)
        sig = jax.nn.sigmoid(gate_f)
        rows = inner[t]
        stage[0, t] = (rows * gate_f * sig).astype(BF16)
        stage[1, t] = (rows * scan_ref[t].astype(F32) * sig * (1.0 + gate_f * (1.0 - sig))).astype(BF16)
    fin = [
        pltpu.make_async_copy(stage.at[0], scan_out, fin_sem.at[0]),
        pltpu.make_async_copy(stage.at[1], gate_out, fin_sem.at[1]),
    ]
    for cp in fin:
        cp.start()

    def drain(c, carry):
        for h in range(2):
            for kind in range(8):
                ag_copy(c, h, kind, send_step(kind)).wait_send()
        return carry

    lax.fori_loop(0, CHUNKS, drain, 0)
    for c in range(CHUNKS - OUTV, CHUNKS):
        out_copy(c).wait()
    for c in (CHUNKS - 2, CHUNKS - 1):
        mate_copy(c).wait_send()
        x_copy(c).wait_send()

    def drain_t(t, carry):
        for k in range(1, 4):
            b1_copy(t, k, False).wait_send()
            d2_copy(t, k, True).wait_recv()
        po_copy(t).wait()
        return carry

    lax.fori_loop(0, MICRO, drain_t, 0)
    for t in (1, 2):
        for k in range(1, 4):
            b2_copy(t, k, False).wait_send()
            d1_copy(t, k, False).wait_send()
            d2_copy(t, k, False).wait_send()
        d2_local(t).wait()

    @pl.when(sec == 1)
    def _():
        for t in range(1, MICRO):
            up_copy(t).wait_send()

    for k in range(1, 4):
        rg_copy(k, False).wait_send()
        ra_copy(k, False).wait_send()
    each_peer(lambda k: rb_copy(k, False).wait_send())
    each_peer(lambda k: rc_copy(k, False).wait_send())
    for cp in fin:
        cp.wait()
    rg_fin.wait()


def layer(inc, hid, eo, routes, routes_t, back, scan, gate, weight, rg):
    vmem = pl.BlockSpec(memory_space=pltpu.VMEM)
    hbm = pl.BlockSpec(memory_space=pl.ANY)
    V = pltpu.VMEM
    DMA = pltpu.SemaphoreType.DMA
    return pl.pallas_call(
        layer_kernel,
        out_shape=(
            jax.ShapeDtypeStruct((MICRO, TOK, WIDTH), BF16),
            jax.ShapeDtypeStruct((MICRO, 256, 512), BF16),
            jax.ShapeDtypeStruct((MICRO, 256, 512), BF16),
            jax.ShapeDtypeStruct((MICRO, SLOTS, WIDTH), BF16),
            jax.ShapeDtypeStruct((512, QB), F32),
            jax.ShapeDtypeStruct((24, QB), F32),
        ),
        in_specs=[hbm, vmem, vmem, vmem, vmem, hbm, vmem, vmem, hbm, vmem],
        out_specs=(hbm,) * 6,
        scratch_shapes=[
            V((CHUNKS, MICRO, 4, 64, CCOL), BF16),
            V((WBUF, 512, CCOL), BF16),
            V((512, 768), BF16),
            V((MICRO, 256, 512), F32),
            V((2, 2, 512, QCOL), F32),
            V((OUTV, 512, QCOL), F32),
            V((2, 2, 512, QCOL), BF16),
            V((CHUNKS, 2, 512, QCOL), BF16),
            V((2, 512, QCOL), BF16),
            V((CHUNKS, 512, QCOL), BF16),
            V((2, MICRO, 256, 512), BF16),
            V((MICRO, TOK, WIDTH), BF16),
            V((MICRO, TOK, WIDTH), BF16),
            V((MICRO, TOK, WIDTH), BF16),
            V((4, 32, QB), BF16),
            V((TOK, WIDTH), F32),
            V((4, 24, QB), F32),
            V((4, 24, QB), F32),
            V((24, QB), F32),
            V((16, 24, 128), F32),
            V((24, QB), F32),
            V((MICRO, SLOTS, WIDTH), BF16),
            V((MICRO, SLOTS, WIDTH), BF16),
            V((2, SLOTS, WIDTH), BF16),
            V((2, SLOTS, WIDTH), BF16),
            V((MICRO, SLOTS, WIDTH), BF16),
            V((2, SLOTS, WIDTH), BF16),
            V((MICRO, TOK, EXPERTS), F32),
            V((MICRO, SLOTS, 1), F32),
            V((MICRO, SLOTS, TOK), BF16),
            V((MICRO, TOK, SLOTS), BF16),
            V((MICRO, TOK, 1), F32),
            DMA((CHUNKS, 2, 8)),
            DMA((CHUNKS, 2, 8)),
            DMA((WBUF,)),
            DMA((CHUNKS,)),
            DMA((CHUNKS,)),
            DMA((CHUNKS,)),
            DMA((CHUNKS,)),
            DMA((CHUNKS,)),
            DMA((3,)),
            DMA((MICRO,)),
        ]
        + [DMA((MICRO, 4))] * 8
        + [DMA((4,))] * 2
        + [DMA((MICRO,))] * 3
        + [DMA((4,))] * 2
        + [DMA((16,))] * 4,
        compiler_params=pltpu.CompilerParams(
            collective_id=0, has_side_effects=True, vmem_limit_bytes=63 * 1024 * 1024
        ),
        cost_estimate=pl.CostEstimate(flops=14_000_000_000, bytes_accessed=30_000_000, transcendentals=0),
    )(inc, hid, eo, routes, routes_t, back, scan, gate, weight, rg)


def on_device(
    incoming, hidden, expert_out, routes, expert_back, scan_out, gate_in, w_out, w_router, norm_gain
):
    rg = jnp.concatenate(
        [w_router[0].T, norm_gain, jnp.zeros((15, w_router.shape[1]), w_router.dtype)], axis=0
    )
    eo = expert_out[0].reshape(MICRO, 2 * TOK, WIDTH)
    passed, scan_grad, gate_grad, expert_grad, weight_grad, small = layer(
        incoming[0], hidden[0], eo, routes[0], jnp.swapaxes(routes[0], 1, 2), expert_back[0],
        scan_out[0], gate_in[0], w_out[0], rg,
    )
    return (
        passed[None],
        scan_grad[None],
        gate_grad[None],
        expert_grad[None],
        weight_grad[None],
        small[:EXPERTS].T[None],
        small[EXPERTS : EXPERTS + 1],
    )


def solution(mesh):
    placed = (
        P("section", None, ("dp", "tensor"), None),
        P("section", None, ("dp", "tensor"), None),
        P("section", None, ("dp", "tensor"), None, None),
        P("section", None, ("dp", "tensor"), None),
        P("section", None, ("dp", "tensor"), None),
        P("section", None, "dp", "tensor"),
        P("section", None, "dp", "tensor"),
        P("section", "tensor", None),
        P("section", "dp", None),
        P("section", "dp"),
    )
    return jax.shard_map(
        on_device,
        mesh=mesh,
        in_specs=placed,
        out_specs=(
            P("section", None, ("dp", "tensor"), None),
            P("section", None, "dp", "tensor"),
            P("section", None, "dp", "tensor"),
            P("section", None, ("dp", "tensor"), None),
            P("section", "tensor", "dp"),
            P("section", "dp", None),
            P("section", "dp"),
        ),
        check_vma=False,
    )
```

```python
import jax
import jax.numpy as jnp
from jax import lax
from jax.experimental import pallas as pl
from jax.experimental.pallas import tpu as pltpu
from jax.sharding import PartitionSpec as P

MESH = pl.DeviceIdType.MESH
MICRO = 3
TOK = 16
WIDTH = 8192
EXPERTS = 16
SLOTS = 64
QB = 2048
CHUNKS = 8
QCOL = 256
CCOL = 1024
HALF = 512
OUTV = 4
WBUF = 3
F32 = jnp.float32
BF16 = jnp.bfloat16


def dot(a, b, dims):
    return lax.dot_general(a, b, ((dims[0], dims[1]), ((), ())), preferred_element_type=F32)


def iota(shape, dim):
    return lax.broadcasted_iota(jnp.int32, shape, dim)


def layer_kernel(
    inc_hbm, hid_hbm, eo_hbm, routes_t_ref, back_hbm, scan_hbm, gate_hbm, w_hbm, wr_ref, gain_ref,
    passed_out, scan_out, gate_out, exp_out, wgrad_out, rg_out,
    G, W, gT, inner, own, outv, msend, mrecv, xsend, xrecv, stage,
    UP, PO, NR, RG, NG, RGA, RA, RB, RBR, RC, BR1, BR2, BP, DS, DR, DP,
    hid_ref, eo_ref, scan_ref, gate_ref, in_sem,
    fw_b1, fw_b2, fw_d1, fw_d2, own_b, own_d,
    probs_s, prob64_s, sel_s, selb_s, inv_s,
    ag_s, ag_r, w_sem, ms_s, ms_r, xs_s, xs_r, out_sem, fin_sem, po_sem,
    b1_s, b1_r, b2_s, b2_r, d1_s, d1_r, d2_s, d2_r, rg_s, rg_r, up_l, up_s, up_r,
    ra_s, ra_r, rb_s, rb_r, rc_s, rc_r,
):
    sec = lax.axis_index("section")
    d = lax.axis_index("dp")
    tau = lax.axis_index("tensor")
    z = tau // 4
    y = tau % 4
    core = d % 2
    xl = d // 2
    mate = xl * 2 + (1 - core)
    xnbr = (1 - xl) * 2 + core

    def at_y(k):
        return z * 4 + (y + k) % 4

    def at_z(k):
        return ((z + k) % 4) * 4 + y

    def al(v, m):
        return pl.multiple_of(v, m)

    def rows16(v):
        return pl.ds(al(16 * v, 16), 16)

    def remote(src, dst, ssem, rsem, peer):
        return pltpu.make_async_remote_copy(
            src_ref=src, dst_ref=dst, send_sem=ssem, recv_sem=rsem, device_id=peer, device_id_type=MESH
        )

    barrier = pltpu.get_barrier_semaphore()

    def greet(k, carry):
        pl.semaphore_signal(barrier, inc=1, device_id={"tensor": (tau + k) % 16}, device_id_type=MESH)
        return carry

    lax.fori_loop(1, 16, greet, 0)
    for k in range(1, 4):
        pl.semaphore_signal(barrier, inc=1, device_id={"dp": (d + k) % 4}, device_id_type=MESH)
    pl.semaphore_signal(barrier, inc=1, device_id={"section": 1 - sec}, device_id_type=MESH)

    loads = [
        pltpu.make_async_copy(src, dst, in_sem.at[n])
        for n, (src, dst) in enumerate(
            ((hid_hbm, hid_ref), (eo_hbm, eo_ref), (scan_hbm, scan_ref), (gate_hbm, gate_ref))
        )
    ]
    for cp in loads:
        cp.start()
    RG[d, 0:EXPERTS, :] = wr_ref[...]
    RG[d, EXPERTS : 2 * EXPERTS, :] = jnp.broadcast_to(
        gain_ref[...].astype(F32), (EXPERTS, QB)
    ).astype(BF16)

    def up_local(t):
        return pltpu.make_async_copy(inc_hbm.at[t], UP.at[t], up_l.at[t])

    up_local(0).start()

    @pl.when(sec == 1)
    def _():
        up_local(1).start()
        up_local(2).start()

    def w_start(c):
        for q in range(4):
            pltpu.make_async_copy(
                w_hbm.at[:, pl.ds(al(q * QB + c * QCOL, QCOL), QCOL)],
                W.at[c % WBUF, :, pl.ds(q * QCOL, QCOL)],
                w_sem.at[c % WBUF],
            ).start()

    class Exchange:
        def __init__(self, src, dst, nbr, coord, fw, ss, rs):
            self.src, self.dst, self.nbr, self.coord = src, dst, nbr, coord
            self.fw, self.ss, self.rs = fw, ss, rs

        def at(self, t, kind, recv):
            def v(k):
                return (self.coord + k) % 4

            low, high, whole = pl.ds(0, WIDTH // 2), pl.ds(WIDTH // 2, WIDTH // 2), pl.ds(0, WIDTH)
            half = (low, high)[kind % 2]
            if kind < 2:
                target = self.fw.at[t, kind]
                source = target if recv else self.src(t, v(2), half)
            elif kind < 4:
                target = self.dst(t, v(3 if kind == 2 else 1) if recv else self.coord, whole)
                source = target if recv else self.src(t, v(1 if kind == 2 else 3), whole)
            else:
                target = self.dst(t, v(2) if recv else v(3 if kind == 4 else 1), half)
                source = target if recv else self.fw.at[t, kind - 4]
            return remote(
                source, target, self.ss.at[t, kind], self.rs.at[t, kind],
                {"tensor": self.nbr(1 if kind % 2 == 0 else 3)},
            )

        def start(self, t):
            for kind in range(4):
                self.at(t, kind, False).start()

        def forward(self, t):
            for kind in range(2):
                self.at(t, kind, True).wait_recv()
                self.at(t, kind + 4, False).start()

        def arrived(self, t):
            for kind in range(2, 6):
                self.at(t, kind, True).wait_recv()

        def sent(self, t):
            for kind in range(4):
                self.at(t, kind, False).wait_send()

        def passed_on(self, t):
            for kind in (4, 5):
                self.at(t, kind, False).wait_send()

    b1 = Exchange(
        lambda t, v, cols: back_hbm.at[t, rows16(v), cols], lambda t, v, cols: BR1.at[t, rows16(v), cols],
        at_z, z, fw_b1, b1_s, b1_r,
    )
    b2 = Exchange(
        lambda t, v, cols: BP.at[t % 2, rows16(v), cols], lambda t, v, cols: BR2.at[t, rows16(v), cols],
        at_y, y, fw_b2, b2_s, b2_r,
    )
    d1 = Exchange(
        lambda t, v, cols: DS.at[t % 2, rows16(v), cols], lambda t, v, cols: DR.at[t, rows16(v), cols],
        at_y, y, fw_d1, d1_s, d1_r,
    )
    d2 = Exchange(
        lambda t, v, cols: DP.at[t % 2, rows16(v), cols], lambda t, v, cols: exp_out.at[t, rows16(v), cols],
        at_z, z, fw_d2, d2_s, d2_r,
    )

    def b1_local(t):
        return pltpu.make_async_copy(back_hbm.at[t, rows16(z)], BR1.at[t, rows16(z)], own_b.at[t])

    def d2_local(t):
        return pltpu.make_async_copy(DP.at[t % 2, rows16(z)], exp_out.at[t, rows16(z)], own_d.at[t])

    def rg_copy(k, recv):
        ref = RG.at[(d + 4 - k) % 4] if recv else RG.at[d]
        return remote(ref, ref, rg_s.at[k], rg_r.at[k], {"dp": (d + k) % 4})

    pl.semaphore_wait(barrier, 19)

    for k in range(1, 4):
        rg_copy(k, False).start()
    for t in range(MICRO):
        b1.start(t)
        b1_local(t).start()
    for c in range(WBUF):
        w_start(c)

    slot_r = iota((SLOTS, TOK), 0)
    slot_e = ((slot_r >> 2) & 3) * 4 + (slot_r >> 4)
    slot_c = slot_r & 3
    slot_rb = iota((TOK, SLOTS), 1)
    slot_eb = ((slot_rb >> 2) & 3) * 4 + (slot_rb >> 4)
    slot_cb = slot_rb & 3
    perm_in = iota((SLOTS, SLOTS), 1)
    perm_out = iota((SLOTS, SLOTS), 0)
    perm = (perm_in == ((perm_out >> 2) & 3) * 16 + (perm_out >> 4) * 4 + (perm_out & 3)).astype(F32).astype(BF16)
    upper = (iota((TOK, TOK), 0) < iota((TOK, TOK), 1)).astype(F32).astype(BF16)
    lower = (iota((TOK, TOK), 0) > iota((TOK, TOK), 1)).astype(F32).astype(BF16)

    eye = iota((TOK, TOK), 0) == iota((TOK, TOK), 1)

    def route_col(t, k):
        row = routes_t_ref[t, k : k + 1, :].astype(F32)
        return jnp.sum(jnp.where(eye, row, 0.0), axis=1, keepdims=True).astype(jnp.int32)

    RGA[...] = jnp.zeros_like(RGA)
    for k in range(1, 4):
        rg_copy(k, True).wait_recv()

    def gain_of(q):
        return RG[q, EXPERTS : EXPERTS + 1, :].astype(F32)

    def hid_of(t, q):
        return hid_ref[t, :, q * QB : (q + 1) * QB].astype(F32)

    def prepare(t, carry):
        total = jnp.zeros((TOK, 1), F32)
        for q in range(4):
            h = hid_of(t, q)
            total += jnp.sum(h * h, axis=1, keepdims=True)
        inv = 1.0 / jnp.sqrt(total / WIDTH + 1e-05)
        inv_s[t] = inv
        logits = jnp.zeros((TOK, EXPERTS), F32)
        logits_t = jnp.zeros((EXPERTS, TOK), F32)
        for q in range(4):
            normed = (hid_of(t, q) * inv * gain_of(q)).astype(BF16)
            NR[t, :, q * QB : (q + 1) * QB] = normed
            router = RG[q, 0:EXPERTS, :]
            logits += dot(normed, router, ((1,), (1,)))
            logits_t += dot(router, normed, ((1,), (1,)))
        weights = jnp.exp(logits)
        probs_s[t] = weights / jnp.sum(weights, axis=1, keepdims=True)
        weights_t = jnp.exp(logits_t)
        probs_t = weights_t / jnp.sum(weights_t, axis=0, keepdims=True)
        spread = jnp.zeros((SLOTS, TOK), F32)
        for e in range(EXPERTS):
            spread = jnp.where(slot_e == e, probs_t[e : e + 1, :], spread)
        rt0 = routes_t_ref[t, 0:1, :]
        rt1 = routes_t_ref[t, 1:2, :]
        named = ((rt0 == slot_e) | (rt1 == slot_e)).astype(F32)
        before = dot(named.astype(BF16), upper, ((1,), (0,)))
        sel = jnp.where(before == slot_c.astype(F32), named, 0.0)
        sel_s[t] = sel.astype(BF16)
        prob64_s[t] = jnp.sum(sel * spread, axis=1, keepdims=True)
        r0 = route_col(t, 0)
        r1 = route_col(t, 1)
        named_b = ((r0 == slot_eb) | (r1 == slot_eb)).astype(F32)
        before_b = dot(lower, named_b.astype(BF16), ((1,), (0,)))
        selb_s[t] = jnp.where(before_b == slot_cb.astype(F32), named_b, 0.0).astype(BF16)
        return carry

    loads[0].wait()
    lax.fori_loop(0, MICRO, prepare, 0)
    for cp in loads[1:]:
        cp.wait()

    def dispatch(t):
        @pl.when(t >= 2)
        def _():
            d1.sent(t - 2)

        prob = prob64_s[t]
        sel = sel_s[t]
        for q in range(4):
            cols = slice(q * QB, (q + 1) * QB)
            DS[t % 2, :, cols] = (dot(sel, UP[t, :, cols], ((1,), (0,))) * prob).astype(BF16)
        d1.start(t)
        DR[t, rows16(y), :] = DS[t % 2, rows16(y), :]

    def dispatch_relay(t):
        d1.arrived(t)

        @pl.when(t >= 2)
        def _():
            d2.sent(t - 2)
            d2_local(t - 2).wait()

        for q in range(4):
            cols = slice(q * QB, (q + 1) * QB)
            DP[t % 2, :, cols] = dot(perm, DR[t, :, cols], ((1,), (0,))).astype(BF16)
        d2.start(t)
        d2_local(t).start()

    def back_relay(t):
        b1.arrived(t)
        b1_local(t).wait()

        @pl.when(t >= 2)
        def _():
            b2.sent(t - 2)

        for q in range(4):
            cols = slice(q * QB, (q + 1) * QB)
            BP[t % 2, :, cols] = dot(perm, BR1[t, :, cols], ((1,), (0,))).astype(BF16)
        b2.start(t)
        BR2[t, rows16(y), :] = BP[t % 2, rows16(y), :]

    def up_copy(t):
        return remote(PO.at[t - 1], UP.at[t], up_s.at[t], up_r.at[t], {"section": 1 - sec})

    def po_copy(t):
        return pltpu.make_async_copy(PO.at[t], passed_out.at[t], po_sem.at[t])

    def upstream_ready(t):
        @pl.when((sec == 1) | (t == 0))
        def _():
            up_local(t).wait()

        @pl.when((sec == 0) & (t > 0))
        def _():
            up_copy(t).wait_recv()

    def combine(t):
        b2.arrived(t)
        scores = jnp.zeros((TOK, 2 * TOK), F32)
        for q in range(4):
            cols = slice(q * QB, (q + 1) * QB)
            scores += dot(UP[t, :, cols], eo_ref[t, :, :, cols].reshape(2 * TOK, QB), ((1,), (1,)))
        row_i = iota((TOK, 2 * TOK), 0)
        col_i = iota((TOK, 2 * TOK), 1)
        s0 = jnp.sum(jnp.where(col_i == 2 * row_i, scores, 0.0), axis=1, keepdims=True)
        s1 = jnp.sum(jnp.where(col_i == 2 * row_i + 1, scores, 0.0), axis=1, keepdims=True)
        expert_i = iota((TOK, EXPERTS), 1)
        prob_grad = jnp.where(route_col(t, 0) == expert_i, s0, 0.0) + jnp.where(
            route_col(t, 1) == expert_i, s1, 0.0
        )
        probs = probs_s[t]
        logit_grad = (
            probs * (prob_grad - jnp.sum(probs * prob_grad, axis=1, keepdims=True))
        ).astype(BF16)
        inv = inv_s[t]
        selb = selb_s[t]
        mean = jnp.zeros((TOK, 1), F32)
        for q in range(4):
            cols = slice(q * QB, (q + 1) * QB)
            norm_grad = dot(logit_grad, RG[q, 0:EXPERTS, :], ((1,), (0,))) + dot(
                selb, BR2[t, :, cols], ((1,), (0,))
            )
            NG[:, cols] = norm_grad
            h = hid_of(t, q)
            mean += jnp.sum(norm_grad * gain_of(q) * h, axis=1, keepdims=True)
            RGA[q, EXPERTS : EXPERTS + 1, :] += jnp.sum(norm_grad * h * inv, axis=0, keepdims=True)
            RGA[q, 0:EXPERTS, :] += dot(logit_grad, NR[t, :, cols], ((0,), (0,)))
        mean = mean / WIDTH
        for q in range(4):
            cols = slice(q * QB, (q + 1) * QB)
            hidden_grad = inv * (NG[:, cols] * gain_of(q)) - hid_of(t, q) * (inv * inv * inv) * mean
            passed = (UP[t, :, cols].astype(F32) + hidden_grad).astype(BF16)
            PO[t, :, cols] = passed
            for c in range(CHUNKS):
                G[c, t, z, rows16(y), q * QCOL : (q + 1) * QCOL] = passed[:, c * QCOL : (c + 1) * QCOL]

        @pl.when((sec == 1) & (t < MICRO - 1))
        def _():
            up_copy(t + 1).start()

        po_copy(t).start()

    upstream_ready(0)

    def front(s, carry):
        @pl.when(s == 0)
        def _():
            dispatch(0)

        @pl.when(s < MICRO)
        def _():
            b1.forward(s)

        @pl.when(s >= 1)
        def _():
            b2.forward(s - 1)

        @pl.when(s < MICRO)
        def _():
            back_relay(s)

        @pl.when(s == 0)
        def _():
            d1.forward(0)

        @pl.when(s == 2)
        def _():
            d2.forward(0)

        @pl.when(s == 3)
        def _():
            d1.forward(1)

        @pl.when(s >= 1)
        def _():
            @pl.when(s >= 2)
            def _():
                upstream_ready(s - 1)

            combine(s - 1)

        @pl.when(s >= 2)
        def _():
            dispatch(s - 1)

        @pl.when((s == 1) | (s == 3))
        def _():
            dispatch_relay((s - 1) // 2)

        return carry

    for t in range(MICRO):
        gate_f = gate_ref[t].astype(F32)
        gated = scan_ref[t].astype(F32) * gate_f * jax.nn.sigmoid(gate_f)
        gT[:, t * 256 : (t + 1) * 256] = gated.T.astype(BF16)
    inner[...] = jnp.zeros_like(inner)
    lax.fori_loop(0, MICRO + 1, front, 0)

    def shard(c, h, k, c0, cw):
        cols = pl.ds(h * HALF + c0, cw)
        if h == 0:
            return G.at[c, :, z, rows16((y + k) % 4), cols]
        return G.at[c, :, (z + k) % 4, rows16(y), cols]

    def block(c, h, k, c0, cw):
        cols = pl.ds(h * HALF + c0, cw)
        if h == 0:
            return G.at[c, :, (z + k) % 4, :, cols]
        return G.at[c, :, :, rows16((y + k) % 4), cols]

    def ag_copy(c, h, kind, k):
        fn = shard if kind < 4 else block
        if kind % 4 < 2:
            ref = fn(c, h, k, 0, HALF)
        else:
            ref = fn(c, h, k, (kind % 2) * (HALF // 2), HALF // 2)
        step = 1 if kind % 2 == 0 else 3
        peer = at_y(step) if (h == 0) == (kind < 4) else at_z(step)
        return remote(ref, ref, ag_s.at[c, h, kind], ag_r.at[c, h, kind], {"tensor": peer})

    def send_step(kind):
        return 0 if kind % 4 < 2 else (3 if kind % 2 == 0 else 1)

    def send(c, h, kind):
        ag_copy(c, h, kind, send_step(kind)).start()

    def recv(c, h, kind):
        step = (3 if kind % 2 == 0 else 1) if kind % 4 < 2 else 2
        ag_copy(c, h, kind, step).wait_recv()

    def t0(c):
        for h in range(2):
            send(c, h, 0)
            send(c, h, 1)

    def t1(c):
        for h in range(2):
            recv(c, h, 0)
            send(c, h, 2)
            recv(c, h, 1)
            send(c, h, 3)

    def t2(c):
        for h in range(2):
            recv(c, h, 2)
            recv(c, h, 3)
            send(c, h, 4)
            send(c, h, 5)

    def t3(c):
        for h in range(2):
            recv(c, h, 4)
            send(c, h, 6)
            recv(c, h, 5)
            send(c, h, 7)

    def mate_copy(c):
        return remote(msend.at[c % 2], mrecv.at[c], ms_s.at[c], ms_r.at[c], {"dp": mate})

    def x_copy(c):
        return remote(xsend.at[c % 2], xrecv.at[c], xs_s.at[c], xs_r.at[c], {"dp": xnbr})

    def out_copy(c):
        return pltpu.make_async_copy(
            outv.at[c % OUTV], wgrad_out.at[:, pl.ds(al(c * QCOL, QCOL), QCOL)], out_sem.at[c]
        )

    def t4(c):
        for h in range(2):
            recv(c, h, 6)
            recv(c, h, 7)
        w_now = W.at[c % WBUF]
        pltpu.make_async_copy(w_now, w_now, w_sem.at[c % WBUF]).wait()
        for t in range(MICRO):
            inner[t] += dot(G[c, t].reshape(256, CCOL), W[c % WBUF], ((1,), (1,)))

        @pl.when(c + WBUF < CHUNKS)
        def _():
            w_start(c + WBUF)

        @pl.when(c >= 2)
        def _():
            mate_copy(c - 2).wait_send()

        for cq in range(2):
            for xq in range(2):
                q = xq * 2 + cq
                cols = slice(q * QCOL, (q + 1) * QCOL)
                part = jnp.zeros((512, QCOL), F32)
                for t in range(MICRO):
                    part += dot(
                        gT[:, t * 256 : (t + 1) * 256], G[c, t, :, :, cols].reshape(256, QCOL), ((1,), (0,))
                    )

                @pl.when(core == cq)
                def _():
                    own[c % 2, xq] = part

                @pl.when(core != cq)
                def _():
                    msend[c % 2, xq] = part.astype(BF16)

        mate_copy(c).start()

    def r1(c):
        mate_copy(c).wait_recv()

        @pl.when(c >= 2)
        def _():
            x_copy(c - 2).wait_send()

        @pl.when(c >= OUTV)
        def _():
            out_copy(c - OUTV).wait()

        xsend[c % 2] = (own[c % 2, 1 - xl] + mrecv[c, 1 - xl].astype(F32)).astype(BF16)
        x_copy(c).start()
        outv[c % OUTV] = own[c % 2, xl] + mrecv[c, xl].astype(F32)

    def r2(c):
        x_copy(c).wait_recv()
        outv[c % OUTV] += xrecv[c].astype(F32)
        out_copy(c).start()

    def ra_copy(k, recv):
        dst = RA.at[(d + 4 - k) % 4] if recv else RA.at[d]
        src = dst if recv else RGA.at[(d + k) % 4]
        return remote(src, dst, ra_s.at[k], ra_r.at[k], {"dp": (d + k) % 4})

    def piece(v):
        return pl.ds(al(128 * v, 128), 128)

    def rb_copy(k, recv):
        dst = RBR.at[(tau + 16 - k) % 16] if recv else RBR.at[tau]
        src = dst if recv else RB.at[:, piece((tau + k) % 16)]
        return remote(src, dst, rb_s.at[k], rb_r.at[k], {"tensor": (tau + k) % 16})

    def rc_copy(k, recv):
        dst = RC.at[:, piece((tau + 16 - k) % 16)] if recv else RC.at[:, piece(tau)]
        return remote(dst, dst, rc_s.at[k], rc_r.at[k], {"tensor": (tau + k) % 16})

    def each_peer(fn):
        def go(k, carry):
            fn(k)
            return carry

        lax.fori_loop(1, 16, go, 0)

    def grads_a():
        for k in range(1, 4):
            ra_copy(k, False).start()
        RA[d] = RGA[d]

    def grads_b():
        for k in range(1, 4):
            ra_copy(k, True).wait_recv()
        RB[...] = RA[0] + RA[1] + RA[2] + RA[3]
        each_peer(lambda k: rb_copy(k, False).start())
        RBR[tau] = RB[:, piece(tau)]

    def grads_c():
        each_peer(lambda k: rb_copy(k, True).wait_recv())
        total = RBR[0]
        for k in range(1, 16):
            total += RBR[k]
        RC[:, piece(tau)] = total
        each_peer(lambda k: rc_copy(k, False).start())

    rg_fin = pltpu.make_async_copy(RC, rg_out, fin_sem.at[2])

    def grads_d():
        each_peer(lambda k: rc_copy(k, True).wait_recv())
        rg_fin.start()

    t0(0)
    grads_a()

    def step(s, carry):
        for lag, fn in ((0, t0), (3, t3), (2, t2), (1, t1), (5, r1), (6, r2), (4, t4)):
            low = lag + (1 if fn is t0 else 0)

            @pl.when((s >= low) & (s < CHUNKS + lag))
            def _():
                fn(s - lag)

        @pl.when(s == 1)
        def _():
            d1.forward(2)
            d2.forward(1)

        @pl.when(s == 2)
        def _():
            dispatch_relay(2)

        @pl.when(s == 4)
        def _():
            d2.forward(2)

        for when, fn in ((2, grads_b), (5, grads_c), (8, grads_d)):

            @pl.when(s == when)
            def _():
                fn()

        return carry

    lax.fori_loop(0, CHUNKS + 7, step, 0)

    for t in range(MICRO):
        gate_f = gate_ref[t].astype(F32)
        sig = jax.nn.sigmoid(gate_f)
        rows = inner[t]
        stage[0, t] = (rows * gate_f * sig).astype(BF16)
        stage[1, t] = (rows * scan_ref[t].astype(F32) * sig * (1.0 + gate_f * (1.0 - sig))).astype(BF16)
    fin = [
        pltpu.make_async_copy(stage.at[0], scan_out, fin_sem.at[0]),
        pltpu.make_async_copy(stage.at[1], gate_out, fin_sem.at[1]),
    ]
    for cp in fin:
        cp.start()

    def drain(c, carry):
        for h in range(2):
            for kind in range(8):
                ag_copy(c, h, kind, send_step(kind)).wait_send()
        return carry

    lax.fori_loop(0, CHUNKS, drain, 0)
    for c in range(CHUNKS - OUTV, CHUNKS):
        out_copy(c).wait()
    for c in (CHUNKS - 2, CHUNKS - 1):
        mate_copy(c).wait_send()
        x_copy(c).wait_send()

    def drain_t(t, carry):
        b1.sent(t)
        d2.arrived(t)
        for ex in (b1, b2, d1, d2):
            ex.passed_on(t)
        po_copy(t).wait()
        return carry

    lax.fori_loop(0, MICRO, drain_t, 0)
    for t in (1, 2):
        b2.sent(t)
        d1.sent(t)
        d2.sent(t)
        d2_local(t).wait()

    @pl.when(sec == 1)
    def _():
        for t in range(1, MICRO):
            up_copy(t).wait_send()

    for k in range(1, 4):
        rg_copy(k, False).wait_send()
        ra_copy(k, False).wait_send()
    each_peer(lambda k: rb_copy(k, False).wait_send())
    each_peer(lambda k: rc_copy(k, False).wait_send())
    for cp in fin:
        cp.wait()
    rg_fin.wait()


def layer(inc, hid, eo, routes_t, back, scan, gate, weight, router, gain):
    vmem = pl.BlockSpec(memory_space=pltpu.VMEM)
    hbm = pl.BlockSpec(memory_space=pl.ANY)
    V = pltpu.VMEM
    DMA = pltpu.SemaphoreType.DMA
    return pl.pallas_call(
        layer_kernel,
        out_shape=(
            jax.ShapeDtypeStruct((MICRO, TOK, WIDTH), BF16),
            jax.ShapeDtypeStruct((MICRO, 256, 512), BF16),
            jax.ShapeDtypeStruct((MICRO, 256, 512), BF16),
            jax.ShapeDtypeStruct((MICRO, SLOTS, WIDTH), BF16),
            jax.ShapeDtypeStruct((512, QB), F32),
            jax.ShapeDtypeStruct((24, QB), F32),
        ),
        in_specs=[hbm, hbm, hbm, vmem, hbm, hbm, hbm, hbm, vmem, vmem],
        out_specs=(hbm,) * 6,
        scratch_shapes=[
            V((CHUNKS, MICRO, 4, 64, CCOL), BF16),
            V((WBUF, 512, CCOL), BF16),
            V((512, 768), BF16),
            V((MICRO, 256, 512), F32),
            V((2, 2, 512, QCOL), F32),
            V((OUTV, 512, QCOL), F32),
            V((2, 2, 512, QCOL), BF16),
            V((CHUNKS, 2, 512, QCOL), BF16),
            V((2, 512, QCOL), BF16),
            V((CHUNKS, 512, QCOL), BF16),
            V((2, MICRO, 256, 512), BF16),
            V((MICRO, TOK, WIDTH), BF16),
            V((MICRO, TOK, WIDTH), BF16),
            V((MICRO, TOK, WIDTH), BF16),
            V((4, 32, QB), BF16),
            V((TOK, WIDTH), F32),
            V((4, 24, QB), F32),
            V((4, 24, QB), F32),
            V((24, QB), F32),
            V((16, 24, 128), F32),
            V((24, QB), F32),
            V((MICRO, SLOTS, WIDTH), BF16),
            V((MICRO, SLOTS, WIDTH), BF16),
            V((2, SLOTS, WIDTH), BF16),
            V((2, SLOTS, WIDTH), BF16),
            V((MICRO, SLOTS, WIDTH), BF16),
            V((2, SLOTS, WIDTH), BF16),
            V((MICRO, TOK, WIDTH), BF16),
            V((MICRO, TOK, 2, WIDTH), BF16),
            V((MICRO, 256, 512), BF16),
            V((MICRO, 256, 512), BF16),
            DMA((4,)),
            V((MICRO, 2, TOK, WIDTH // 2), BF16),
            V((MICRO, 2, TOK, WIDTH // 2), BF16),
            V((MICRO, 2, TOK, WIDTH // 2), BF16),
            V((MICRO, 2, TOK, WIDTH // 2), BF16),
            DMA((MICRO,)),
            DMA((MICRO,)),
            V((MICRO, TOK, EXPERTS), F32),
            V((MICRO, SLOTS, 1), F32),
            V((MICRO, SLOTS, TOK), BF16),
            V((MICRO, TOK, SLOTS), BF16),
            V((MICRO, TOK, 1), F32),
            DMA((CHUNKS, 2, 8)),
            DMA((CHUNKS, 2, 8)),
            DMA((WBUF,)),
            DMA((CHUNKS,)),
            DMA((CHUNKS,)),
            DMA((CHUNKS,)),
            DMA((CHUNKS,)),
            DMA((CHUNKS,)),
            DMA((3,)),
            DMA((MICRO,)),
        ]
        + [DMA((MICRO, 6))] * 8
        + [DMA((4,))] * 2
        + [DMA((MICRO,))] * 3
        + [DMA((4,))] * 2
        + [DMA((16,))] * 4,
        compiler_params=pltpu.CompilerParams(
            collective_id=0, has_side_effects=True, vmem_limit_bytes=63 * 1024 * 1024
        ),
        cost_estimate=pl.CostEstimate(flops=14_000_000_000, bytes_accessed=30_000_000, transcendentals=0),
    )(inc, hid, eo, routes_t, back, scan, gate, weight, router, gain)


def finish_kernel(*refs):
    sems = refs[-1]
    small, router, gain = refs[5], refs[11], refs[12]
    copies = [pltpu.make_async_copy(refs[n], refs[6 + n], sems.at[n]) for n in range(5)]
    for cp in copies:
        cp.start()
    router[...] = small[0:EXPERTS, :]
    gain[...] = small[EXPERTS : EXPERTS + 1, :]
    for cp in copies:
        cp.wait()


def finish(arrays):
    vmem = pl.BlockSpec(memory_space=pltpu.VMEM)
    hbm = pl.BlockSpec(memory_space=pl.ANY)
    return pl.pallas_call(
        finish_kernel,
        out_shape=tuple(jax.ShapeDtypeStruct(a.shape, a.dtype) for a in arrays[:5])
        + (jax.ShapeDtypeStruct((EXPERTS, QB), F32), jax.ShapeDtypeStruct((1, QB), F32)),
        in_specs=[hbm] * 5 + [vmem],
        out_specs=(hbm,) * 5 + (vmem, vmem),
        scratch_shapes=[pltpu.SemaphoreType.DMA((5,))],
        cost_estimate=pl.CostEstimate(flops=0, bytes_accessed=20_000_000, transcendentals=0),
    )(*arrays)


def on_device(
    incoming, hidden, expert_out, routes, expert_back, scan_out, gate_in, w_out, w_router, norm_gain
):
    outs = layer(
        incoming[0], hidden[0], expert_out[0], jnp.swapaxes(routes[0], 1, 2), expert_back[0],
        scan_out[0], gate_in[0], w_out[0], w_router[0].T, norm_gain,
    )
    passed, scan_grad, gate_grad, expert_grad, weight_grad, router, gain = finish(outs)
    return (
        passed[None],
        scan_grad[None],
        gate_grad[None],
        expert_grad[None],
        weight_grad[None],
        router.T[None],
        gain,
    )


def solution(mesh):
    placed = (
        P("section", None, ("dp", "tensor"), None),
        P("section", None, ("dp", "tensor"), None),
        P("section", None, ("dp", "tensor"), None, None),
        P("section", None, ("dp", "tensor"), None),
        P("section", None, ("dp", "tensor"), None),
        P("section", None, "dp", "tensor"),
        P("section", None, "dp", "tensor"),
        P("section", "tensor", None),
        P("section", "dp", None),
        P("section", "dp"),
    )
    return jax.shard_map(
        on_device,
        mesh=mesh,
        in_specs=placed,
        out_specs=(
            P("section", None, ("dp", "tensor"), None),
            P("section", None, "dp", "tensor"),
            P("section", None, "dp", "tensor"),
            P("section", None, ("dp", "tensor"), None),
            P("section", "tensor", "dp"),
            P("section", "dp", None),
            P("section", "dp"),
        ),
        check_vma=False,
    )
```

```python
import jax
import jax.numpy as jnp
from jax import lax
from jax.experimental import pallas as pl
from jax.experimental.pallas import tpu as pltpu
from jax.sharding import PartitionSpec as P

MESH = pl.DeviceIdType.MESH
MICRO = 3
TOK = 16
WIDTH = 8192
EXPERTS = 16
SLOTS = 64
QB = 2048
CHUNKS = 8
QCOL = 256
CCOL = 1024
HALF = 512
OUTV = 4
WBUF = 2
F32 = jnp.float32
BF16 = jnp.bfloat16


def dot(a, b, dims):
    return lax.dot_general(a, b, ((dims[0], dims[1]), ((), ())), preferred_element_type=F32)


def iota(shape, dim):
    return lax.broadcasted_iota(jnp.int32, shape, dim)


def layer_kernel(
    inc_hbm, hid_hbm, eo_hbm, routes_t_ref, back_hbm, scan_hbm, gate_hbm, w_hbm, wr_ref, gain_ref,
    passed_out, scan_out, gate_out, exp_out, wgrad_out, rg_out,
    G, W, gT, inner, own, outv, msend, mrecv, xsend, xrecv, stage,
    UP, PO, NR, RG, NG, RGA, RA, RB, RBR, RC, BR1, BR2, BP, DS, DR, DP,
    hid_ref, eo_ref, scan_ref, gate_ref, in_sem,
    EB, DX, eb_sem, dx_sem,
    probs_s, prob64_s, sel_s, selb_s, inv_s,
    ag_s, ag_r, w_sem, ms_s, ms_r, xs_s, xs_r, out_sem, fin_sem, po_sem,
    b1_s, b1_r, b2_s, b2_r, d1_s, d1_r, d2_s, d2_r, rg_s, rg_r, up_l, up_s, up_r,
    ra_s, ra_r, rb_s, rb_r, rc_s, rc_r,
):
    sec = lax.axis_index("section")
    d = lax.axis_index("dp")
    tau = lax.axis_index("tensor")
    z = tau // 4
    y = tau % 4
    core = d % 2
    xl = d // 2
    mate = xl * 2 + (1 - core)
    xnbr = (1 - xl) * 2 + core

    def at_y(k):
        return z * 4 + (y + k) % 4

    def at_z(k):
        return ((z + k) % 4) * 4 + y

    def al(v, m):
        return pl.multiple_of(v, m)

    def rows16(v):
        return pl.ds(al(16 * v, 16), 16)

    def remote(src, dst, ssem, rsem, peer):
        return pltpu.make_async_remote_copy(
            src_ref=src, dst_ref=dst, send_sem=ssem, recv_sem=rsem, device_id=peer, device_id_type=MESH
        )

    barrier = pltpu.get_barrier_semaphore()

    def greet(k, carry):
        pl.semaphore_signal(barrier, inc=1, device_id={"tensor": (tau + k) % 16}, device_id_type=MESH)
        return carry

    lax.fori_loop(1, 16, greet, 0)
    for k in range(1, 4):
        pl.semaphore_signal(barrier, inc=1, device_id={"dp": (d + k) % 4}, device_id_type=MESH)
    pl.semaphore_signal(barrier, inc=1, device_id={"section": 1 - sec}, device_id_type=MESH)

    loads = [
        pltpu.make_async_copy(src, dst, in_sem.at[n])
        for n, (src, dst) in enumerate(
            ((hid_hbm, hid_ref), (eo_hbm, eo_ref), (scan_hbm, scan_ref), (gate_hbm, gate_ref))
        )
    ]
    eb_loads = [pltpu.make_async_copy(back_hbm.at[t], EB.at[t], eb_sem.at[t]) for t in range(MICRO)]
    for cp in eb_loads + loads:
        cp.start()
    RG[d, 0:EXPERTS, :] = wr_ref[...]
    RG[d, EXPERTS : 2 * EXPERTS, :] = jnp.broadcast_to(
        gain_ref[...].astype(F32), (EXPERTS, QB)
    ).astype(BF16)

    def up_local(t):
        return pltpu.make_async_copy(inc_hbm.at[t], UP.at[t], up_l.at[t])

    up_local(0).start()

    @pl.when(sec == 1)
    def _():
        up_local(1).start()
        up_local(2).start()

    def w_start(c):
        for q in range(4):
            pltpu.make_async_copy(
                w_hbm.at[:, pl.ds(al(q * QB + c * QCOL, QCOL), QCOL)],
                W.at[c % WBUF, :, pl.ds(q * QCOL, QCOL)],
                w_sem.at[c % WBUF],
            ).start()

    def b1_copy(t, k, recv):
        if recv:
            ref = BR1.at[t, rows16((z + 4 - k) % 4)]
            return remote(ref, ref, b1_s.at[t, k], b1_r.at[t, k], {"tensor": at_z(k)})
        return remote(
            EB.at[t, rows16((z + k) % 4)], BR1.at[t, rows16(z)],
            b1_s.at[t, k], b1_r.at[t, k], {"tensor": at_z(k)},
        )

    def b1_local(t):
        return pltpu.make_async_copy(EB.at[t, rows16(z)], BR1.at[t, rows16(z)], b1_r.at[t, 0])

    def b2_copy(t, k, recv):
        if recv:
            ref = BR2.at[t, rows16((y + 4 - k) % 4)]
            return remote(ref, ref, b2_s.at[t, k], b2_r.at[t, k], {"tensor": at_y(k)})
        return remote(
            BP.at[t % 2, rows16((y + k) % 4)], BR2.at[t, rows16(y)],
            b2_s.at[t, k], b2_r.at[t, k], {"tensor": at_y(k)},
        )

    def d1_copy(t, k, recv):
        if recv:
            ref = DR.at[t, rows16((y + 4 - k) % 4)]
            return remote(ref, ref, d1_s.at[t, k], d1_r.at[t, k], {"tensor": at_y(k)})
        return remote(
            DS.at[t % 2, rows16((y + k) % 4)], DR.at[t, rows16(y)],
            d1_s.at[t, k], d1_r.at[t, k], {"tensor": at_y(k)},
        )

    def d2_copy(t, k, recv):
        if recv:
            ref = DX.at[t, rows16((z + 4 - k) % 4)]
            return remote(ref, ref, d2_s.at[t, k], d2_r.at[t, k], {"tensor": at_z(k)})
        return remote(
            DP.at[t % 2, rows16((z + k) % 4)], DX.at[t, rows16(z)],
            d2_s.at[t, k], d2_r.at[t, k], {"tensor": at_z(k)},
        )

    def d2_local(t):
        return pltpu.make_async_copy(DP.at[t % 2, rows16(z)], DX.at[t, rows16(z)], d2_r.at[t, 0])

    def rg_copy(k, recv):
        ref = RG.at[(d + 4 - k) % 4] if recv else RG.at[d]
        return remote(ref, ref, rg_s.at[k], rg_r.at[k], {"dp": (d + k) % 4})

    pl.semaphore_wait(barrier, 19)

    for k in range(1, 4):
        rg_copy(k, False).start()
    for t in range(MICRO):
        eb_loads[t].wait()
        for k in (2, 1, 3):
            b1_copy(t, k, False).start()
        b1_local(t).start()
    for c in range(WBUF):
        w_start(c)

    slot_r = iota((SLOTS, TOK), 0)
    slot_e = ((slot_r >> 2) & 3) * 4 + (slot_r >> 4)
    slot_c = slot_r & 3
    slot_rb = iota((TOK, SLOTS), 1)
    slot_eb = ((slot_rb >> 2) & 3) * 4 + (slot_rb >> 4)
    slot_cb = slot_rb & 3
    perm_in = iota((SLOTS, SLOTS), 1)
    perm_out = iota((SLOTS, SLOTS), 0)
    perm = (perm_in == ((perm_out >> 2) & 3) * 16 + (perm_out >> 4) * 4 + (perm_out & 3)).astype(F32).astype(BF16)
    upper = (iota((TOK, TOK), 0) < iota((TOK, TOK), 1)).astype(F32).astype(BF16)
    lower = (iota((TOK, TOK), 0) > iota((TOK, TOK), 1)).astype(F32).astype(BF16)

    eye = iota((TOK, TOK), 0) == iota((TOK, TOK), 1)

    def route_col(t, k):
        row = routes_t_ref[t, k : k + 1, :].astype(F32)
        return jnp.sum(jnp.where(eye, row, 0.0), axis=1, keepdims=True).astype(jnp.int32)

    RGA[...] = jnp.zeros_like(RGA)
    for k in range(1, 4):
        rg_copy(k, True).wait_recv()

    def gain_of(q):
        return RG[q, EXPERTS : EXPERTS + 1, :].astype(F32)

    def hid_of(t, q):
        return hid_ref[t, :, q * QB : (q + 1) * QB].astype(F32)

    def prepare(t, carry):
        total = jnp.zeros((TOK, 1), F32)
        for q in range(4):
            h = hid_of(t, q)
            total += jnp.sum(h * h, axis=1, keepdims=True)
        inv = 1.0 / jnp.sqrt(total / WIDTH + 1e-05)
        inv_s[t] = inv
        logits = jnp.zeros((TOK, EXPERTS), F32)
        logits_t = jnp.zeros((EXPERTS, TOK), F32)
        for q in range(4):
            normed = (hid_of(t, q) * inv * gain_of(q)).astype(BF16)
            NR[t, :, q * QB : (q + 1) * QB] = normed
            router = RG[q, 0:EXPERTS, :]
            logits += dot(normed, router, ((1,), (1,)))
            logits_t += dot(router, normed, ((1,), (1,)))
        weights = jnp.exp(logits)
        probs_s[t] = weights / jnp.sum(weights, axis=1, keepdims=True)
        weights_t = jnp.exp(logits_t)
        probs_t = weights_t / jnp.sum(weights_t, axis=0, keepdims=True)
        spread = jnp.zeros((SLOTS, TOK), F32)
        for e in range(EXPERTS):
            spread = jnp.where(slot_e == e, probs_t[e : e + 1, :], spread)
        rt0 = routes_t_ref[t, 0:1, :]
        rt1 = routes_t_ref[t, 1:2, :]
        named = ((rt0 == slot_e) | (rt1 == slot_e)).astype(F32)
        before = dot(named.astype(BF16), upper, ((1,), (0,)))
        sel = jnp.where(before == slot_c.astype(F32), named, 0.0)
        sel_s[t] = sel.astype(BF16)
        prob64_s[t] = jnp.sum(sel * spread, axis=1, keepdims=True)
        r0 = route_col(t, 0)
        r1 = route_col(t, 1)
        named_b = ((r0 == slot_eb) | (r1 == slot_eb)).astype(F32)
        before_b = dot(lower, named_b.astype(BF16), ((1,), (0,)))
        selb_s[t] = jnp.where(before_b == slot_cb.astype(F32), named_b, 0.0).astype(BF16)
        return carry

    loads[0].wait()
    lax.fori_loop(0, MICRO, prepare, 0)
    for cp in loads[1:]:
        cp.wait()

    def dispatch(t):
        @pl.when(t >= 2)
        def _():
            for k in range(1, 4):
                d1_copy(t - 2, k, False).wait_send()

        prob = prob64_s[t]
        sel = sel_s[t]
        for q in range(4):
            cols = slice(q * QB, (q + 1) * QB)
            DS[t % 2, :, cols] = (dot(sel, UP[t, :, cols], ((1,), (0,))) * prob).astype(BF16)
        for k in (2, 1, 3):
            d1_copy(t, k, False).start()
        DR[t, rows16(y), :] = DS[t % 2, rows16(y), :]

    def dispatch_relay(t):
        for k in range(1, 4):
            d1_copy(t, k, True).wait_recv()

        @pl.when(t >= 2)
        def _():
            for k in range(1, 4):
                d2_copy(t - 2, k, False).wait_send()
            d2_local(t - 2).wait()

        for q in range(4):
            cols = slice(q * QB, (q + 1) * QB)
            DP[t % 2, :, cols] = dot(perm, DR[t, :, cols], ((1,), (0,))).astype(BF16)
        for k in (2, 1, 3):
            d2_copy(t, k, False).start()
        d2_local(t).start()

    def back_relay(t):
        for k in range(1, 4):
            b1_copy(t, k, True).wait_recv()
        b1_local(t).wait()

        @pl.when(t >= 2)
        def _():
            for k in range(1, 4):
                b2_copy(t - 2, k, False).wait_send()

        for q in range(4):
            cols = slice(q * QB, (q + 1) * QB)
            BP[t % 2, :, cols] = dot(perm, BR1[t, :, cols], ((1,), (0,))).astype(BF16)
        for k in (2, 1, 3):
            b2_copy(t, k, False).start()
        BR2[t, rows16(y), :] = BP[t % 2, rows16(y), :]

    def up_copy(t):
        return remote(PO.at[t - 1], UP.at[t], up_s.at[t], up_r.at[t], {"section": 1 - sec})

    def po_copy(t):
        return pltpu.make_async_copy(PO.at[t], passed_out.at[t], po_sem.at[t])

    def upstream_ready(t):
        @pl.when((sec == 1) | (t == 0))
        def _():
            up_local(t).wait()

        @pl.when((sec == 0) & (t > 0))
        def _():
            up_copy(t).wait_recv()

    def combine(t):
        for k in range(1, 4):
            b2_copy(t, k, True).wait_recv()
        scores = jnp.zeros((TOK, 2 * TOK), F32)
        for q in range(4):
            cols = slice(q * QB, (q + 1) * QB)
            scores += dot(UP[t, :, cols], eo_ref[t, :, :, cols].reshape(2 * TOK, QB), ((1,), (1,)))
        row_i = iota((TOK, 2 * TOK), 0)
        col_i = iota((TOK, 2 * TOK), 1)
        s0 = jnp.sum(jnp.where(col_i == 2 * row_i, scores, 0.0), axis=1, keepdims=True)
        s1 = jnp.sum(jnp.where(col_i == 2 * row_i + 1, scores, 0.0), axis=1, keepdims=True)
        expert_i = iota((TOK, EXPERTS), 1)
        prob_grad = jnp.where(route_col(t, 0) == expert_i, s0, 0.0) + jnp.where(
            route_col(t, 1) == expert_i, s1, 0.0
        )
        probs = probs_s[t]
        logit_grad = (
            probs * (prob_grad - jnp.sum(probs * prob_grad, axis=1, keepdims=True))
        ).astype(BF16)
        inv = inv_s[t]
        selb = selb_s[t]
        mean = jnp.zeros((TOK, 1), F32)
        for q in range(4):
            cols = slice(q * QB, (q + 1) * QB)
            norm_grad = dot(logit_grad, RG[q, 0:EXPERTS, :], ((1,), (0,))) + dot(
                selb, BR2[t, :, cols], ((1,), (0,))
            )
            NG[:, cols] = norm_grad
            h = hid_of(t, q)
            mean += jnp.sum(norm_grad * gain_of(q) * h, axis=1, keepdims=True)
            RGA[q, EXPERTS : EXPERTS + 1, :] += jnp.sum(norm_grad * h * inv, axis=0, keepdims=True)
            RGA[q, 0:EXPERTS, :] += dot(logit_grad, NR[t, :, cols], ((0,), (0,)))
        mean = mean / WIDTH
        for q in range(4):
            cols = slice(q * QB, (q + 1) * QB)
            hidden_grad = inv * (NG[:, cols] * gain_of(q)) - hid_of(t, q) * (inv * inv * inv) * mean
            passed = (UP[t, :, cols].astype(F32) + hidden_grad).astype(BF16)
            PO[t, :, cols] = passed
            for c in range(CHUNKS):
                G[c, t, z, rows16(y), q * QCOL : (q + 1) * QCOL] = passed[:, c * QCOL : (c + 1) * QCOL]

        @pl.when((sec == 1) & (t < MICRO - 1))
        def _():
            up_copy(t + 1).start()

        po_copy(t).start()

    upstream_ready(0)

    def front(s, carry):
        @pl.when(s == 0)
        def _():
            dispatch(0)

        @pl.when(s < MICRO)
        def _():
            back_relay(s)

        @pl.when(s >= 1)
        def _():
            @pl.when(s >= 2)
            def _():
                upstream_ready(s - 1)

            combine(s - 1)

        @pl.when(s >= 2)
        def _():
            dispatch(s - 1)

        @pl.when((s == 1) | (s == 3))
        def _():
            dispatch_relay((s - 1) // 2)

        return carry

    for t in range(MICRO):
        gate_f = gate_ref[t].astype(F32)
        gated = scan_ref[t].astype(F32) * gate_f * jax.nn.sigmoid(gate_f)
        gT[:, t * 256 : (t + 1) * 256] = gated.T.astype(BF16)
    inner[...] = jnp.zeros_like(inner)
    lax.fori_loop(0, MICRO + 1, front, 0)

    def shard(c, h, k, c0, cw):
        cols = pl.ds(h * HALF + c0, cw)
        if h == 0:
            return G.at[c, :, z, rows16((y + k) % 4), cols]
        return G.at[c, :, (z + k) % 4, rows16(y), cols]

    def block(c, h, k, c0, cw):
        cols = pl.ds(h * HALF + c0, cw)
        if h == 0:
            return G.at[c, :, (z + k) % 4, :, cols]
        return G.at[c, :, :, rows16((y + k) % 4), cols]

    def ag_copy(c, h, kind, k):
        fn = shard if kind < 4 else block
        if kind % 4 < 2:
            ref = fn(c, h, k, 0, HALF)
        else:
            ref = fn(c, h, k, (kind % 2) * (HALF // 2), HALF // 2)
        step = 1 if kind % 2 == 0 else 3
        peer = at_y(step) if (h == 0) == (kind < 4) else at_z(step)
        return remote(ref, ref, ag_s.at[c, h, kind], ag_r.at[c, h, kind], {"tensor": peer})

    def send_step(kind):
        return 0 if kind % 4 < 2 else (3 if kind % 2 == 0 else 1)

    def send(c, h, kind):
        ag_copy(c, h, kind, send_step(kind)).start()

    def recv(c, h, kind):
        step = (3 if kind % 2 == 0 else 1) if kind % 4 < 2 else 2
        ag_copy(c, h, kind, step).wait_recv()

    def t0(c):
        for h in range(2):
            send(c, h, 0)
            send(c, h, 1)

    def t1(c):
        for h in range(2):
            recv(c, h, 0)
            send(c, h, 2)
            recv(c, h, 1)
            send(c, h, 3)

    def t2(c):
        for h in range(2):
            recv(c, h, 2)
            recv(c, h, 3)
            send(c, h, 4)
            send(c, h, 5)

    def t3(c):
        for h in range(2):
            recv(c, h, 4)
            send(c, h, 6)
            recv(c, h, 5)
            send(c, h, 7)

    def mate_copy(c):
        return remote(msend.at[c % 2], mrecv.at[c], ms_s.at[c], ms_r.at[c], {"dp": mate})

    def x_copy(c):
        return remote(xsend.at[c % 2], xrecv.at[c], xs_s.at[c], xs_r.at[c], {"dp": xnbr})

    def out_copy(c):
        return pltpu.make_async_copy(
            outv.at[c % OUTV], wgrad_out.at[:, pl.ds(al(c * QCOL, QCOL), QCOL)], out_sem.at[c]
        )

    def t4(c):
        for h in range(2):
            recv(c, h, 6)
            recv(c, h, 7)
        w_now = W.at[c % WBUF]
        pltpu.make_async_copy(w_now, w_now, w_sem.at[c % WBUF]).wait()
        for t in range(MICRO):
            inner[t] += dot(G[c, t].reshape(256, CCOL), W[c % WBUF], ((1,), (1,)))

        @pl.when(c + WBUF < CHUNKS)
        def _():
            w_start(c + WBUF)

        @pl.when(c >= 2)
        def _():
            mate_copy(c - 2).wait_send()

        for cq in range(2):
            for xq in range(2):
                q = xq * 2 + cq
                cols = slice(q * QCOL, (q + 1) * QCOL)
                part = jnp.zeros((512, QCOL), F32)
                for t in range(MICRO):
                    part += dot(
                        gT[:, t * 256 : (t + 1) * 256], G[c, t, :, :, cols].reshape(256, QCOL), ((1,), (0,))
                    )

                @pl.when(core == cq)
                def _():
                    own[c % 2, xq] = part

                @pl.when(core != cq)
                def _():
                    msend[c % 2, xq] = part.astype(BF16)

        mate_copy(c).start()

    def r1(c):
        mate_copy(c).wait_recv()

        @pl.when(c >= 2)
        def _():
            x_copy(c - 2).wait_send()

        @pl.when(c >= OUTV)
        def _():
            out_copy(c - OUTV).wait()

        xsend[c % 2] = (own[c % 2, 1 - xl] + mrecv[c, 1 - xl].astype(F32)).astype(BF16)
        x_copy(c).start()
        outv[c % OUTV] = own[c % 2, xl] + mrecv[c, xl].astype(F32)

    def r2(c):
        x_copy(c).wait_recv()
        outv[c % OUTV] += xrecv[c].astype(F32)
        out_copy(c).start()

    def ra_copy(k, recv):
        dst = RA.at[(d + 4 - k) % 4] if recv else RA.at[d]
        src = dst if recv else RGA.at[(d + k) % 4]
        return remote(src, dst, ra_s.at[k], ra_r.at[k], {"dp": (d + k) % 4})

    def piece(v):
        return pl.ds(al(128 * v, 128), 128)

    def rb_copy(k, recv):
        dst = RBR.at[(tau + 16 - k) % 16] if recv else RBR.at[tau]
        src = dst if recv else RB.at[:, piece((tau + k) % 16)]
        return remote(src, dst, rb_s.at[k], rb_r.at[k], {"tensor": (tau + k) % 16})

    def rc_copy(k, recv):
        dst = RC.at[:, piece((tau + 16 - k) % 16)] if recv else RC.at[:, piece(tau)]
        return remote(dst, dst, rc_s.at[k], rc_r.at[k], {"tensor": (tau + k) % 16})

    def each_peer(fn):
        def go(k, carry):
            fn(k)
            return carry

        lax.fori_loop(1, 16, go, 0)

    def grads_a():
        for k in range(1, 4):
            ra_copy(k, False).start()
        RA[d] = RGA[d]

    def grads_b():
        for k in range(1, 4):
            ra_copy(k, True).wait_recv()
        RB[...] = RA[0] + RA[1] + RA[2] + RA[3]
        each_peer(lambda k: rb_copy(k, False).start())
        RBR[tau] = RB[:, piece(tau)]

    def grads_c():
        each_peer(lambda k: rb_copy(k, True).wait_recv())
        total = RBR[0]
        for k in range(1, 16):
            total += RBR[k]
        RC[:, piece(tau)] = total
        each_peer(lambda k: rc_copy(k, False).start())

    rg_fin = pltpu.make_async_copy(RC, rg_out, fin_sem.at[2])

    def grads_d():
        each_peer(lambda k: rc_copy(k, True).wait_recv())
        rg_fin.start()

    t0(0)
    grads_a()

    fin = [
        pltpu.make_async_copy(stage.at[0], scan_out, fin_sem.at[0]),
        pltpu.make_async_copy(stage.at[1], gate_out, fin_sem.at[1]),
    ]

    def finish_mixer():
        for t in range(MICRO):
            gate_f = gate_ref[t].astype(F32)
            sig = jax.nn.sigmoid(gate_f)
            rows = inner[t]
            stage[0, t] = (rows * gate_f * sig).astype(BF16)
            stage[1, t] = (rows * scan_ref[t].astype(F32) * sig * (1.0 + gate_f * (1.0 - sig))).astype(BF16)
        for cp in fin:
            cp.start()

    def dx_copy(t):
        return pltpu.make_async_copy(DX.at[t], exp_out.at[t], dx_sem.at[t])

    def step(s, carry):
        for lag, fn in ((0, t0), (3, t3), (2, t2), (1, t1), (5, r1), (6, r2), (4, t4)):
            low = lag + (1 if fn is t0 else 0)

            @pl.when((s >= low) & (s < CHUNKS + lag))
            def _():
                fn(s - lag)

        @pl.when(s == 1)
        def _():
            dispatch_relay(2)

        for when, fn in ((2, grads_b), (5, grads_c), (8, grads_d)):

            @pl.when(s == when)
            def _():
                fn()

        @pl.when(s == CHUNKS + 4)
        def _():
            finish_mixer()

        return carry

    lax.fori_loop(0, CHUNKS + 6, step, 0)
    for t in range(MICRO):
        for k in range(1, 4):
            d2_copy(t, k, True).wait_recv()
        if t >= 1:
            d2_local(t).wait()
        dx_copy(t).start()

    def drain(c, carry):
        for h in range(2):
            for kind in range(8):
                ag_copy(c, h, kind, send_step(kind)).wait_send()
        return carry

    lax.fori_loop(0, CHUNKS, drain, 0)
    for c in range(CHUNKS - OUTV, CHUNKS):
        out_copy(c).wait()
    for c in (CHUNKS - 2, CHUNKS - 1):
        mate_copy(c).wait_send()
        x_copy(c).wait_send()

    def drain_t(t, carry):
        for k in range(1, 4):
            b1_copy(t, k, False).wait_send()
        po_copy(t).wait()
        return carry

    lax.fori_loop(0, MICRO, drain_t, 0)
    for t in (1, 2):
        for k in range(1, 4):
            b2_copy(t, k, False).wait_send()
            d1_copy(t, k, False).wait_send()
            d2_copy(t, k, False).wait_send()

    @pl.when(sec == 1)
    def _():
        for t in range(1, MICRO):
            up_copy(t).wait_send()

    for k in range(1, 4):
        rg_copy(k, False).wait_send()
        ra_copy(k, False).wait_send()
    each_peer(lambda k: rb_copy(k, False).wait_send())
    each_peer(lambda k: rc_copy(k, False).wait_send())
    for cp in fin:
        cp.wait()
    for t in range(MICRO):
        dx_copy(t).wait()
    rg_fin.wait()


def layer(inc, hid, eo, routes_t, back, scan, gate, weight, router, gain):
    vmem = pl.BlockSpec(memory_space=pltpu.VMEM)
    hbm = pl.BlockSpec(memory_space=pl.ANY)
    V = pltpu.VMEM
    DMA = pltpu.SemaphoreType.DMA
    return pl.pallas_call(
        layer_kernel,
        out_shape=(
            jax.ShapeDtypeStruct((MICRO, TOK, WIDTH), BF16),
            jax.ShapeDtypeStruct((MICRO, 256, 512), BF16),
            jax.ShapeDtypeStruct((MICRO, 256, 512), BF16),
            jax.ShapeDtypeStruct((MICRO, SLOTS, WIDTH), BF16),
            jax.ShapeDtypeStruct((512, QB), F32),
            jax.ShapeDtypeStruct((24, QB), F32),
        ),
        in_specs=[hbm, hbm, hbm, vmem, hbm, hbm, hbm, hbm, vmem, vmem],
        out_specs=(hbm,) * 6,
        scratch_shapes=[
            V((CHUNKS, MICRO, 4, 64, CCOL), BF16),
            V((WBUF, 512, CCOL), BF16),
            V((512, 768), BF16),
            V((MICRO, 256, 512), F32),
            V((2, 2, 512, QCOL), F32),
            V((OUTV, 512, QCOL), F32),
            V((2, 2, 512, QCOL), BF16),
            V((CHUNKS, 2, 512, QCOL), BF16),
            V((2, 512, QCOL), BF16),
            V((CHUNKS, 512, QCOL), BF16),
            V((2, MICRO, 256, 512), BF16),
            V((MICRO, TOK, WIDTH), BF16),
            V((MICRO, TOK, WIDTH), BF16),
            V((MICRO, TOK, WIDTH), BF16),
            V((4, 32, QB), BF16),
            V((TOK, WIDTH), F32),
            V((4, 24, QB), F32),
            V((4, 24, QB), F32),
            V((24, QB), F32),
            V((16, 24, 128), F32),
            V((24, QB), F32),
            V((MICRO, SLOTS, WIDTH), BF16),
            V((MICRO, SLOTS, WIDTH), BF16),
            V((2, SLOTS, WIDTH), BF16),
            V((2, SLOTS, WIDTH), BF16),
            V((MICRO, SLOTS, WIDTH), BF16),
            V((2, SLOTS, WIDTH), BF16),
            V((MICRO, TOK, WIDTH), BF16),
            V((MICRO, TOK, 2, WIDTH), BF16),
            V((MICRO, 256, 512), BF16),
            V((MICRO, 256, 512), BF16),
            DMA((4,)),
            V((MICRO, SLOTS, WIDTH), BF16),
            V((MICRO, SLOTS, WIDTH), BF16),
            DMA((MICRO,)),
            DMA((MICRO,)),
            V((MICRO, TOK, EXPERTS), F32),
            V((MICRO, SLOTS, 1), F32),
            V((MICRO, SLOTS, TOK), BF16),
            V((MICRO, TOK, SLOTS), BF16),
            V((MICRO, TOK, 1), F32),
            DMA((CHUNKS, 2, 8)),
            DMA((CHUNKS, 2, 8)),
            DMA((WBUF,)),
            DMA((CHUNKS,)),
            DMA((CHUNKS,)),
            DMA((CHUNKS,)),
            DMA((CHUNKS,)),
            DMA((CHUNKS,)),
            DMA((3,)),
            DMA((MICRO,)),
        ]
        + [DMA((MICRO, 4))] * 8
        + [DMA((4,))] * 2
        + [DMA((MICRO,))] * 3
        + [DMA((4,))] * 2
        + [DMA((16,))] * 4,
        compiler_params=pltpu.CompilerParams(
            collective_id=0, has_side_effects=True, vmem_limit_bytes=63 * 1024 * 1024
        ),
        cost_estimate=pl.CostEstimate(flops=14_000_000_000, bytes_accessed=30_000_000, transcendentals=0),
    )(inc, hid, eo, routes_t, back, scan, gate, weight, router, gain)


def finish_kernel(*refs):
    small, router, gain = refs[5], refs[11], refs[12]
    stages, sems = refs[13:18], refs[18]
    loads = [pltpu.make_async_copy(refs[n], stages[n], sems.at[0, n]) for n in range(5)]
    stores = [pltpu.make_async_copy(stages[n], refs[6 + n], sems.at[1, n]) for n in range(5)]
    for cp in loads:
        cp.start()
    router[...] = small[0:EXPERTS, :]
    gain[...] = small[EXPERTS : EXPERTS + 1, :]
    for load, store in zip(loads, stores):
        load.wait()
        store.start()
    for cp in stores:
        cp.wait()


def finish(arrays):
    vmem = pl.BlockSpec(memory_space=pltpu.VMEM)
    hbm = pl.BlockSpec(memory_space=pl.ANY)
    return pl.pallas_call(
        finish_kernel,
        out_shape=tuple(jax.ShapeDtypeStruct(a.shape, a.dtype) for a in arrays[:5])
        + (jax.ShapeDtypeStruct((EXPERTS, QB), F32), jax.ShapeDtypeStruct((1, QB), F32)),
        in_specs=[hbm] * 5 + [vmem],
        out_specs=(hbm,) * 5 + (vmem, vmem),
        scratch_shapes=[pltpu.VMEM(a.shape, a.dtype) for a in arrays[:5]]
        + [pltpu.SemaphoreType.DMA((2, 5))],
        compiler_params=pltpu.CompilerParams(vmem_limit_bytes=32 * 1024 * 1024),
        cost_estimate=pl.CostEstimate(flops=0, bytes_accessed=20_000_000, transcendentals=0),
    )(*arrays)


def on_device(
    incoming, hidden, expert_out, routes, expert_back, scan_out, gate_in, w_out, w_router, norm_gain
):
    outs = layer(
        incoming[0], hidden[0], expert_out[0], jnp.swapaxes(routes[0], 1, 2), expert_back[0],
        scan_out[0], gate_in[0], w_out[0], w_router[0].T, norm_gain,
    )
    passed, scan_grad, gate_grad, expert_grad, weight_grad, router, gain = finish(outs)
    return (
        passed[None],
        scan_grad[None],
        gate_grad[None],
        expert_grad[None],
        weight_grad[None],
        router.T[None],
        gain,
    )


def solution(mesh):
    placed = (
        P("section", None, ("dp", "tensor"), None),
        P("section", None, ("dp", "tensor"), None),
        P("section", None, ("dp", "tensor"), None, None),
        P("section", None, ("dp", "tensor"), None),
        P("section", None, ("dp", "tensor"), None),
        P("section", None, "dp", "tensor"),
        P("section", None, "dp", "tensor"),
        P("section", "tensor", None),
        P("section", "dp", None),
        P("section", "dp"),
    )
    return jax.shard_map(
        on_device,
        mesh=mesh,
        in_specs=placed,
        out_specs=(
            P("section", None, ("dp", "tensor"), None),
            P("section", None, "dp", "tensor"),
            P("section", None, "dp", "tensor"),
            P("section", None, ("dp", "tensor"), None),
            P("section", "tensor", "dp"),
            P("section", "dp", None),
            P("section", "dp"),
        ),
        check_vma=False,
    )
```

```python
import jax
import jax.numpy as jnp
from jax import lax
from jax.experimental import pallas as pl
from jax.experimental.pallas import tpu as pltpu
from jax.sharding import PartitionSpec as P

MESH = pl.DeviceIdType.MESH
MICRO = 3
TOK = 16
WIDTH = 8192
EXPERTS = 16
SLOTS = 64
QB = 2048
CHUNKS = 8
QCOL = 256
CCOL = 1024
HALF = 512
OUTV = 4
WBUF = 2
F32 = jnp.float32
BF16 = jnp.bfloat16


def dot(a, b, dims):
    return lax.dot_general(a, b, ((dims[0], dims[1]), ((), ())), preferred_element_type=F32)


def iota(shape, dim):
    return lax.broadcasted_iota(jnp.int32, shape, dim)


def layer_kernel(
    inc_hbm, hid_hbm, eo_hbm, routes_t_ref, back_hbm, scan_hbm, gate_hbm, w_hbm, wr_ref, gain_ref,
    passed_out, scan_out, gate_out, exp_out, wgrad_out, rg_out,
    G, W, gT, inner, own, outv, msend, mrecv, xsend, xrecv, stage,
    UP, PO, NR, RG, NG, RGA, RA, RB, RBR, RC, BR1, BR2, BP, DS, DR, DP,
    hid_ref, eo_ref, scan_ref, gate_ref, in_sem,
    EB, DX, eb_sem, dx_sem,
    probs_s, prob64_s, sel_s, selb_s, inv_s,
    ag_s, ag_r, w_sem, ms_s, ms_r, xs_s, xs_r, out_sem, fin_sem, po_sem,
    b1_s, b1_r, b2_s, b2_r, d1_s, d1_r, d2_s, d2_r, rg_s, rg_r, up_l, up_s, up_r,
    ra_s, ra_r, rb_s, rb_r, rc_s, rc_r,
):
    sec = lax.axis_index("section")
    d = lax.axis_index("dp")
    tau = lax.axis_index("tensor")
    z = tau // 4
    y = tau % 4
    core = d % 2
    xl = d // 2
    mate = xl * 2 + (1 - core)
    xnbr = (1 - xl) * 2 + core

    def at_y(k):
        return z * 4 + (y + k) % 4

    def at_z(k):
        return ((z + k) % 4) * 4 + y

    def al(v, m):
        return pl.multiple_of(v, m)

    def rows16(v):
        return pl.ds(al(16 * v, 16), 16)

    def remote(src, dst, ssem, rsem, peer):
        return pltpu.make_async_remote_copy(
            src_ref=src, dst_ref=dst, send_sem=ssem, recv_sem=rsem, device_id=peer, device_id_type=MESH
        )

    barrier = pltpu.get_barrier_semaphore()

    def greet(k, carry):
        pl.semaphore_signal(barrier, inc=1, device_id={"tensor": (tau + k) % 16}, device_id_type=MESH)
        return carry

    lax.fori_loop(1, 16, greet, 0)
    for k in range(1, 4):
        pl.semaphore_signal(barrier, inc=1, device_id={"dp": (d + k) % 4}, device_id_type=MESH)
    pl.semaphore_signal(barrier, inc=1, device_id={"section": 1 - sec}, device_id_type=MESH)

    loads = [
        pltpu.make_async_copy(src, dst, in_sem.at[n])
        for n, (src, dst) in enumerate(
            ((hid_hbm, hid_ref), (eo_hbm, eo_ref), (scan_hbm, scan_ref), (gate_hbm, gate_ref))
        )
    ]
    eb_loads = [pltpu.make_async_copy(back_hbm.at[t], EB.at[t], eb_sem.at[t]) for t in range(MICRO)]
    for cp in eb_loads + loads:
        cp.start()
    RG[d, 0:EXPERTS, :] = wr_ref[...]
    RG[d, EXPERTS : 2 * EXPERTS, :] = jnp.broadcast_to(
        gain_ref[...].astype(F32), (EXPERTS, QB)
    ).astype(BF16)

    def up_local(t):
        return pltpu.make_async_copy(inc_hbm.at[t], UP.at[t], up_l.at[t])

    up_local(0).start()

    @pl.when(sec == 1)
    def _():
        up_local(1).start()
        up_local(2).start()

    def w_start(c):
        for q in range(4):
            pltpu.make_async_copy(
                w_hbm.at[:, pl.ds(al(q * QB + c * QCOL, QCOL), QCOL)],
                W.at[c % WBUF, :, pl.ds(q * QCOL, QCOL)],
                w_sem.at[c % WBUF],
            ).start()

    def b1_copy(t, k, recv):
        if recv:
            ref = BR1.at[t, rows16((z + 4 - k) % 4)]
            return remote(ref, ref, b1_s.at[t, k], b1_r.at[t, k], {"tensor": at_z(k)})
        return remote(
            EB.at[t, rows16((z + k) % 4)], BR1.at[t, rows16(z)],
            b1_s.at[t, k], b1_r.at[t, k], {"tensor": at_z(k)},
        )

    def b1_local(t):
        return pltpu.make_async_copy(EB.at[t, rows16(z)], BR1.at[t, rows16(z)], b1_r.at[t, 0])

    def b2_copy(t, k, recv):
        if recv:
            ref = BR2.at[t, rows16((y + 4 - k) % 4)]
            return remote(ref, ref, b2_s.at[t, k], b2_r.at[t, k], {"tensor": at_y(k)})
        return remote(
            BP.at[t % 2, rows16((y + k) % 4)], BR2.at[t, rows16(y)],
            b2_s.at[t, k], b2_r.at[t, k], {"tensor": at_y(k)},
        )

    def d1_copy(t, k, recv):
        if recv:
            ref = DR.at[t, rows16((y + 4 - k) % 4)]
            return remote(ref, ref, d1_s.at[t, k], d1_r.at[t, k], {"tensor": at_y(k)})
        return remote(
            DS.at[t % 2, rows16((y + k) % 4)], DR.at[t, rows16(y)],
            d1_s.at[t, k], d1_r.at[t, k], {"tensor": at_y(k)},
        )

    def d2_copy(t, k, recv):
        if recv:
            ref = DX.at[t, rows16((z + 4 - k) % 4)]
            return remote(ref, ref, d2_s.at[t, k], d2_r.at[t, k], {"tensor": at_z(k)})
        return remote(
            DP.at[t % 2, rows16((z + k) % 4)], DX.at[t, rows16(z)],
            d2_s.at[t, k], d2_r.at[t, k], {"tensor": at_z(k)},
        )

    def d2_local(t):
        return pltpu.make_async_copy(DP.at[t % 2, rows16(z)], DX.at[t, rows16(z)], d2_r.at[t, 0])

    def rg_copy(k, recv):
        ref = RG.at[(d + 4 - k) % 4] if recv else RG.at[d]
        return remote(ref, ref, rg_s.at[k], rg_r.at[k], {"dp": (d + k) % 4})

    pl.semaphore_wait(barrier, 19)

    for k in range(1, 4):
        rg_copy(k, False).start()
    for t in range(MICRO):
        eb_loads[t].wait()
        for k in (2, 1, 3):
            b1_copy(t, k, False).start()
        b1_local(t).start()
    for c in range(WBUF):
        w_start(c)

    slot_r = iota((SLOTS, TOK), 0)
    slot_e = ((slot_r >> 2) & 3) * 4 + (slot_r >> 4)
    slot_c = slot_r & 3
    slot_rb = iota((TOK, SLOTS), 1)
    slot_eb = ((slot_rb >> 2) & 3) * 4 + (slot_rb >> 4)
    slot_cb = slot_rb & 3
    perm_in = iota((SLOTS, SLOTS), 1)
    perm_out = iota((SLOTS, SLOTS), 0)
    perm = (perm_in == ((perm_out >> 2) & 3) * 16 + (perm_out >> 4) * 4 + (perm_out & 3)).astype(F32).astype(BF16)
    upper = (iota((TOK, TOK), 0) < iota((TOK, TOK), 1)).astype(F32).astype(BF16)
    lower = (iota((TOK, TOK), 0) > iota((TOK, TOK), 1)).astype(F32).astype(BF16)

    eye = iota((TOK, TOK), 0) == iota((TOK, TOK), 1)

    def route_col(t, k):
        row = routes_t_ref[t, k : k + 1, :].astype(F32)
        return jnp.sum(jnp.where(eye, row, 0.0), axis=1, keepdims=True).astype(jnp.int32)

    RGA[...] = jnp.zeros_like(RGA)
    for k in range(1, 4):
        rg_copy(k, True).wait_recv()

    def gain_of(q):
        return RG[q, EXPERTS : EXPERTS + 1, :].astype(F32)

    def hid_of(t, q):
        return hid_ref[t, :, q * QB : (q + 1) * QB].astype(F32)

    def prepare(t, carry):
        total = jnp.zeros((TOK, 1), F32)
        for q in range(4):
            h = hid_of(t, q)
            total += jnp.sum(h * h, axis=1, keepdims=True)
        inv = 1.0 / jnp.sqrt(total / WIDTH + 1e-05)
        inv_s[t] = inv
        logits = jnp.zeros((TOK, EXPERTS), F32)
        logits_t = jnp.zeros((EXPERTS, TOK), F32)
        for q in range(4):
            normed = (hid_of(t, q) * inv * gain_of(q)).astype(BF16)
            NR[t, :, q * QB : (q + 1) * QB] = normed
            router = RG[q, 0:EXPERTS, :]
            logits += dot(normed, router, ((1,), (1,)))
            logits_t += dot(router, normed, ((1,), (1,)))
        weights = jnp.exp(logits)
        probs_s[t] = weights / jnp.sum(weights, axis=1, keepdims=True)
        weights_t = jnp.exp(logits_t)
        probs_t = weights_t / jnp.sum(weights_t, axis=0, keepdims=True)
        spread = jnp.zeros((SLOTS, TOK), F32)
        for e in range(EXPERTS):
            spread = jnp.where(slot_e == e, probs_t[e : e + 1, :], spread)
        rt0 = routes_t_ref[t, 0:1, :]
        rt1 = routes_t_ref[t, 1:2, :]
        named = ((rt0 == slot_e) | (rt1 == slot_e)).astype(F32)
        before = dot(named.astype(BF16), upper, ((1,), (0,)))
        sel = jnp.where(before == slot_c.astype(F32), named, 0.0)
        sel_s[t] = sel.astype(BF16)
        prob64_s[t] = jnp.sum(sel * spread, axis=1, keepdims=True)
        r0 = route_col(t, 0)
        r1 = route_col(t, 1)
        named_b = ((r0 == slot_eb) | (r1 == slot_eb)).astype(F32)
        before_b = dot(lower, named_b.astype(BF16), ((1,), (0,)))
        selb_s[t] = jnp.where(before_b == slot_cb.astype(F32), named_b, 0.0).astype(BF16)
        return carry

    loads[0].wait()
    lax.fori_loop(0, MICRO, prepare, 0)
    for cp in loads[1:]:
        cp.wait()

    def dispatch(t):
        @pl.when(t >= 2)
        def _():
            for k in range(1, 4):
                d1_copy(t - 2, k, False).wait_send()

        prob = prob64_s[t]
        sel = sel_s[t]
        for q in range(4):
            cols = slice(q * QB, (q + 1) * QB)
            DS[t % 2, :, cols] = (dot(sel, UP[t, :, cols], ((1,), (0,))) * prob).astype(BF16)
        for k in (2, 1, 3):
            d1_copy(t, k, False).start()
        DR[t, rows16(y), :] = DS[t % 2, rows16(y), :]

    def dispatch_relay(t):
        for k in range(1, 4):
            d1_copy(t, k, True).wait_recv()

        @pl.when(t >= 2)
        def _():
            for k in range(1, 4):
                d2_copy(t - 2, k, False).wait_send()
            d2_local(t - 2).wait()

        for q in range(4):
            cols = slice(q * QB, (q + 1) * QB)
            DP[t % 2, :, cols] = dot(perm, DR[t, :, cols], ((1,), (0,))).astype(BF16)
        for k in (2, 1, 3):
            d2_copy(t, k, False).start()
        d2_local(t).start()

    def back_relay(t):
        for k in range(1, 4):
            b1_copy(t, k, True).wait_recv()
        b1_local(t).wait()

        @pl.when(t >= 2)
        def _():
            for k in range(1, 4):
                b2_copy(t - 2, k, False).wait_send()

        for q in range(4):
            cols = slice(q * QB, (q + 1) * QB)
            BP[t % 2, :, cols] = dot(perm, BR1[t, :, cols], ((1,), (0,))).astype(BF16)
        for k in (2, 1, 3):
            b2_copy(t, k, False).start()
        BR2[t, rows16(y), :] = BP[t % 2, rows16(y), :]

    def up_copy(t):
        return remote(PO.at[t - 1], UP.at[t], up_s.at[t], up_r.at[t], {"section": 1 - sec})

    def po_copy(t):
        return pltpu.make_async_copy(PO.at[t], passed_out.at[t], po_sem.at[t])

    def upstream_ready(t):
        @pl.when((sec == 1) | (t == 0))
        def _():
            up_local(t).wait()

        @pl.when((sec == 0) & (t > 0))
        def _():
            up_copy(t).wait_recv()

    def combine(t):
        for k in range(1, 4):
            b2_copy(t, k, True).wait_recv()
        scores = jnp.zeros((TOK, 2 * TOK), F32)
        for q in range(4):
            cols = slice(q * QB, (q + 1) * QB)
            scores += dot(UP[t, :, cols], eo_ref[t, :, :, cols].reshape(2 * TOK, QB), ((1,), (1,)))
        row_i = iota((TOK, 2 * TOK), 0)
        col_i = iota((TOK, 2 * TOK), 1)
        s0 = jnp.sum(jnp.where(col_i == 2 * row_i, scores, 0.0), axis=1, keepdims=True)
        s1 = jnp.sum(jnp.where(col_i == 2 * row_i + 1, scores, 0.0), axis=1, keepdims=True)
        expert_i = iota((TOK, EXPERTS), 1)
        prob_grad = jnp.where(route_col(t, 0) == expert_i, s0, 0.0) + jnp.where(
            route_col(t, 1) == expert_i, s1, 0.0
        )
        probs = probs_s[t]
        logit_grad = (
            probs * (prob_grad - jnp.sum(probs * prob_grad, axis=1, keepdims=True))
        ).astype(BF16)
        inv = inv_s[t]
        selb = selb_s[t]
        mean = jnp.zeros((TOK, 1), F32)
        for q in range(4):
            cols = slice(q * QB, (q + 1) * QB)
            norm_grad = dot(logit_grad, RG[q, 0:EXPERTS, :], ((1,), (0,))) + dot(
                selb, BR2[t, :, cols], ((1,), (0,))
            )
            NG[:, cols] = norm_grad
            h = hid_of(t, q)
            mean += jnp.sum(norm_grad * gain_of(q) * h, axis=1, keepdims=True)
            RGA[q, EXPERTS : EXPERTS + 1, :] += jnp.sum(norm_grad * h * inv, axis=0, keepdims=True)
            RGA[q, 0:EXPERTS, :] += dot(logit_grad, NR[t, :, cols], ((0,), (0,)))
        mean = mean / WIDTH
        for q in range(4):
            cols = slice(q * QB, (q + 1) * QB)
            hidden_grad = inv * (NG[:, cols] * gain_of(q)) - hid_of(t, q) * (inv * inv * inv) * mean
            passed = (UP[t, :, cols].astype(F32) + hidden_grad).astype(BF16)
            PO[t, :, cols] = passed
            for c in range(CHUNKS):
                G[c, t, z, rows16(y), q * QCOL : (q + 1) * QCOL] = passed[:, c * QCOL : (c + 1) * QCOL]

        @pl.when((sec == 1) & (t < MICRO - 1))
        def _():
            up_copy(t + 1).start()

        po_copy(t).start()

    upstream_ready(0)

    def front(s, carry):
        @pl.when(s == 0)
        def _():
            dispatch(0)

        @pl.when(s < MICRO)
        def _():
            back_relay(s)

        @pl.when(s >= 1)
        def _():
            @pl.when(s >= 2)
            def _():
                upstream_ready(s - 1)

            combine(s - 1)

        @pl.when(s >= 2)
        def _():
            dispatch(s - 1)

        @pl.when((s == 1) | (s == 3))
        def _():
            dispatch_relay((s - 1) // 2)

        return carry

    for t in range(MICRO):
        gate_f = gate_ref[t].astype(F32)
        gated = scan_ref[t].astype(F32) * gate_f * jax.nn.sigmoid(gate_f)
        gT[:, t * 256 : (t + 1) * 256] = gated.T.astype(BF16)
    inner[...] = jnp.zeros_like(inner)
    lax.fori_loop(0, MICRO + 1, front, 0)

    def shard(c, h, k, c0, cw):
        cols = pl.ds(h * HALF + c0, cw)
        if h == 0:
            return G.at[c, :, z, rows16((y + k) % 4), cols]
        return G.at[c, :, (z + k) % 4, rows16(y), cols]

    def block(c, h, k, c0, cw):
        cols = pl.ds(h * HALF + c0, cw)
        if h == 0:
            return G.at[c, :, (z + k) % 4, :, cols]
        return G.at[c, :, :, rows16((y + k) % 4), cols]

    def ag_copy(c, h, kind, k):
        fn = shard if kind < 4 else block
        if kind % 4 < 2:
            ref = fn(c, h, k, 0, HALF)
        else:
            ref = fn(c, h, k, (kind % 2) * (HALF // 2), HALF // 2)
        step = 1 if kind % 2 == 0 else 3
        peer = at_y(step) if (h == 0) == (kind < 4) else at_z(step)
        return remote(ref, ref, ag_s.at[c, h, kind], ag_r.at[c, h, kind], {"tensor": peer})

    def send_step(kind):
        return 0 if kind % 4 < 2 else (3 if kind % 2 == 0 else 1)

    def send(c, h, kind):
        ag_copy(c, h, kind, send_step(kind)).start()

    def recv(c, h, kind):
        step = (3 if kind % 2 == 0 else 1) if kind % 4 < 2 else 2
        ag_copy(c, h, kind, step).wait_recv()

    def t0(c):
        for h in range(2):
            send(c, h, 0)
            send(c, h, 1)

    def t1(c):
        for h in range(2):
            recv(c, h, 0)
            send(c, h, 2)
            recv(c, h, 1)
            send(c, h, 3)

    def t2(c):
        for h in range(2):
            recv(c, h, 2)
            recv(c, h, 3)
            send(c, h, 4)
            send(c, h, 5)

    def t3(c):
        for h in range(2):
            recv(c, h, 4)
            send(c, h, 6)
            recv(c, h, 5)
            send(c, h, 7)

    def mate_copy(c):
        return remote(msend.at[c % 2], mrecv.at[c], ms_s.at[c], ms_r.at[c], {"dp": mate})

    def x_copy(c):
        return remote(xsend.at[c % 2], xrecv.at[c], xs_s.at[c], xs_r.at[c], {"dp": xnbr})

    def out_copy(c):
        return pltpu.make_async_copy(
            outv.at[c % OUTV], wgrad_out.at[:, pl.ds(al(c * QCOL, QCOL), QCOL)], out_sem.at[c]
        )

    def t4(c):
        for h in range(2):
            recv(c, h, 6)
            recv(c, h, 7)
        w_now = W.at[c % WBUF]
        pltpu.make_async_copy(w_now, w_now, w_sem.at[c % WBUF]).wait()
        for t in range(MICRO):
            inner[t] += dot(G[c, t].reshape(256, CCOL), W[c % WBUF], ((1,), (1,)))

        @pl.when(c + WBUF < CHUNKS)
        def _():
            w_start(c + WBUF)

        @pl.when(c >= 2)
        def _():
            mate_copy(c - 2).wait_send()

        for cq in range(2):
            for xq in range(2):
                q = xq * 2 + cq
                cols = slice(q * QCOL, (q + 1) * QCOL)
                part = jnp.zeros((512, QCOL), F32)
                for t in range(MICRO):
                    part += dot(
                        gT[:, t * 256 : (t + 1) * 256], G[c, t, :, :, cols].reshape(256, QCOL), ((1,), (0,))
                    )

                @pl.when(core == cq)
                def _():
                    own[c % 2, xq] = part

                @pl.when(core != cq)
                def _():
                    msend[c % 2, xq] = part.astype(BF16)

        mate_copy(c).start()

    def r1(c):
        mate_copy(c).wait_recv()

        @pl.when(c >= 2)
        def _():
            x_copy(c - 2).wait_send()

        @pl.when(c >= OUTV)
        def _():
            out_copy(c - OUTV).wait()

        xsend[c % 2] = (own[c % 2, 1 - xl] + mrecv[c, 1 - xl].astype(F32)).astype(BF16)
        x_copy(c).start()
        outv[c % OUTV] = own[c % 2, xl] + mrecv[c, xl].astype(F32)

    def r2(c):
        x_copy(c).wait_recv()
        outv[c % OUTV] += xrecv[c].astype(F32)
        out_copy(c).start()

    def ra_copy(k, recv):
        dst = RA.at[(d + 4 - k) % 4] if recv else RA.at[d]
        src = dst if recv else RGA.at[(d + k) % 4]
        return remote(src, dst, ra_s.at[k], ra_r.at[k], {"dp": (d + k) % 4})

    def piece(v):
        return pl.ds(al(128 * v, 128), 128)

    def rb_copy(k, recv):
        dst = RBR.at[(tau + 16 - k) % 16] if recv else RBR.at[tau]
        src = dst if recv else RB.at[:, piece((tau + k) % 16)]
        return remote(src, dst, rb_s.at[k], rb_r.at[k], {"tensor": (tau + k) % 16})

    def rc_copy(k, recv):
        dst = RC.at[:, piece((tau + 16 - k) % 16)] if recv else RC.at[:, piece(tau)]
        return remote(dst, dst, rc_s.at[k], rc_r.at[k], {"tensor": (tau + k) % 16})

    def each_peer(fn):
        def go(k, carry):
            fn(k)
            return carry

        lax.fori_loop(1, 16, go, 0)

    def grads_a():
        for k in range(1, 4):
            ra_copy(k, False).start()
        RA[d] = RGA[d]

    def grads_b():
        for k in range(1, 4):
            ra_copy(k, True).wait_recv()
        RB[...] = RA[0] + RA[1] + RA[2] + RA[3]
        each_peer(lambda k: rb_copy(k, False).start())
        RBR[tau] = RB[:, piece(tau)]

    def grads_c():
        each_peer(lambda k: rb_copy(k, True).wait_recv())
        total = RBR[0]
        for k in range(1, 16):
            total += RBR[k]
        RC[:, piece(tau)] = total
        each_peer(lambda k: rc_copy(k, False).start())

    rg_fin = pltpu.make_async_copy(RC, rg_out, fin_sem.at[2])

    def grads_d():
        each_peer(lambda k: rc_copy(k, True).wait_recv())
        rg_fin.start()

    t0(0)
    grads_a()

    fin = [
        pltpu.make_async_copy(stage.at[0], scan_out, fin_sem.at[0]),
        pltpu.make_async_copy(stage.at[1], gate_out, fin_sem.at[1]),
    ]

    def finish_mixer():
        for t in range(MICRO):
            gate_f = gate_ref[t].astype(F32)
            sig = jax.nn.sigmoid(gate_f)
            rows = inner[t]
            stage[0, t] = (rows * gate_f * sig).astype(BF16)
            stage[1, t] = (rows * scan_ref[t].astype(F32) * sig * (1.0 + gate_f * (1.0 - sig))).astype(BF16)
        for cp in fin:
            cp.start()

    def dx_copy(t):
        return pltpu.make_async_copy(DX.at[t], exp_out.at[t], dx_sem.at[t])

    def step(s, carry):
        for lag, fn in ((0, t0), (3, t3), (2, t2), (1, t1), (5, r1), (6, r2), (4, t4)):
            low = lag + (1 if fn is t0 else 0)

            @pl.when((s >= low) & (s < CHUNKS + lag))
            def _():
                fn(s - lag)

        @pl.when(s == 1)
        def _():
            dispatch_relay(2)

        for when, fn in ((2, grads_b), (5, grads_c), (8, grads_d)):

            @pl.when(s == when)
            def _():
                fn()

        @pl.when(s == CHUNKS + 4)
        def _():
            finish_mixer()

        return carry

    lax.fori_loop(0, CHUNKS + 6, step, 0)
    for t in range(MICRO):
        for k in range(1, 4):
            d2_copy(t, k, True).wait_recv()
        if t >= 1:
            d2_local(t).wait()
        dx_copy(t).start()

    def drain(c, carry):
        for h in range(2):
            for kind in range(8):
                ag_copy(c, h, kind, send_step(kind)).wait_send()
        return carry

    lax.fori_loop(0, CHUNKS, drain, 0)
    for c in range(CHUNKS - OUTV, CHUNKS):
        out_copy(c).wait()
    for c in (CHUNKS - 2, CHUNKS - 1):
        mate_copy(c).wait_send()
        x_copy(c).wait_send()

    def drain_t(t, carry):
        for k in range(1, 4):
            b1_copy(t, k, False).wait_send()
        po_copy(t).wait()
        return carry

    lax.fori_loop(0, MICRO, drain_t, 0)
    for t in (1, 2):
        for k in range(1, 4):
            b2_copy(t, k, False).wait_send()
            d1_copy(t, k, False).wait_send()
            d2_copy(t, k, False).wait_send()

    @pl.when(sec == 1)
    def _():
        for t in range(1, MICRO):
            up_copy(t).wait_send()

    for k in range(1, 4):
        rg_copy(k, False).wait_send()
        ra_copy(k, False).wait_send()
    each_peer(lambda k: rb_copy(k, False).wait_send())
    each_peer(lambda k: rc_copy(k, False).wait_send())
    for cp in fin:
        cp.wait()
    for t in range(MICRO):
        dx_copy(t).wait()
    rg_fin.wait()


def layer(inc, hid, eo, routes_t, back, scan, gate, weight, router, gain):
    vmem = pl.BlockSpec(memory_space=pltpu.VMEM)
    hbm = pl.BlockSpec(memory_space=pl.ANY)
    V = pltpu.VMEM
    DMA = pltpu.SemaphoreType.DMA
    return pl.pallas_call(
        layer_kernel,
        out_shape=(
            jax.ShapeDtypeStruct((MICRO, TOK, WIDTH), BF16),
            jax.ShapeDtypeStruct((MICRO, 256, 512), BF16),
            jax.ShapeDtypeStruct((MICRO, 256, 512), BF16),
            jax.ShapeDtypeStruct((MICRO, SLOTS, WIDTH), BF16),
            jax.ShapeDtypeStruct((512, QB), F32),
            jax.ShapeDtypeStruct((24, QB), F32),
        ),
        in_specs=[hbm, hbm, hbm, vmem, hbm, hbm, hbm, hbm, vmem, vmem],
        out_specs=(hbm,) * 6,
        scratch_shapes=[
            V((CHUNKS, MICRO, 4, 64, CCOL), BF16),
            V((WBUF, 512, CCOL), BF16),
            V((512, 768), BF16),
            V((MICRO, 256, 512), F32),
            V((2, 2, 512, QCOL), F32),
            V((OUTV, 512, QCOL), F32),
            V((2, 2, 512, QCOL), BF16),
            V((CHUNKS, 2, 512, QCOL), BF16),
            V((2, 512, QCOL), BF16),
            V((CHUNKS, 512, QCOL), BF16),
            V((2, MICRO, 256, 512), BF16),
            V((MICRO, TOK, WIDTH), BF16),
            V((MICRO, TOK, WIDTH), BF16),
            V((MICRO, TOK, WIDTH), BF16),
            V((4, 32, QB), BF16),
            V((TOK, WIDTH), F32),
            V((4, 24, QB), F32),
            V((4, 24, QB), F32),
            V((24, QB), F32),
            V((16, 24, 128), F32),
            V((24, QB), F32),
            V((MICRO, SLOTS, WIDTH), BF16),
            V((MICRO, SLOTS, WIDTH), BF16),
            V((2, SLOTS, WIDTH), BF16),
            V((2, SLOTS, WIDTH), BF16),
            V((MICRO, SLOTS, WIDTH), BF16),
            V((2, SLOTS, WIDTH), BF16),
            V((MICRO, TOK, WIDTH), BF16),
            V((MICRO, TOK, 2, WIDTH), BF16),
            V((MICRO, 256, 512), BF16),
            V((MICRO, 256, 512), BF16),
            DMA((4,)),
            V((MICRO, SLOTS, WIDTH), BF16),
            V((MICRO, SLOTS, WIDTH), BF16),
            DMA((MICRO,)),
            DMA((MICRO,)),
            V((MICRO, TOK, EXPERTS), F32),
            V((MICRO, SLOTS, 1), F32),
            V((MICRO, SLOTS, TOK), BF16),
            V((MICRO, TOK, SLOTS), BF16),
            V((MICRO, TOK, 1), F32),
            DMA((CHUNKS, 2, 8)),
            DMA((CHUNKS, 2, 8)),
            DMA((WBUF,)),
            DMA((CHUNKS,)),
            DMA((CHUNKS,)),
            DMA((CHUNKS,)),
            DMA((CHUNKS,)),
            DMA((CHUNKS,)),
            DMA((3,)),
            DMA((MICRO,)),
        ]
        + [DMA((MICRO, 4))] * 8
        + [DMA((4,))] * 2
        + [DMA((MICRO,))] * 3
        + [DMA((4,))] * 2
        + [DMA((16,))] * 4,
        compiler_params=pltpu.CompilerParams(
            collective_id=0, has_side_effects=True, vmem_limit_bytes=63 * 1024 * 1024
        ),
        cost_estimate=pl.CostEstimate(flops=14_000_000_000, bytes_accessed=30_000_000, transcendentals=0),
    )(inc, hid, eo, routes_t, back, scan, gate, weight, router, gain)


def finish_kernel(*refs):
    small, router, gain = refs[5], refs[11], refs[12]
    stages, sems = refs[13:18], refs[18]
    loads = [pltpu.make_async_copy(refs[n], stages[n], sems.at[0, n]) for n in range(5)]
    stores = [pltpu.make_async_copy(stages[n], refs[6 + n], sems.at[1, n]) for n in range(5)]
    for cp in loads:
        cp.start()
    router[...] = small[0:EXPERTS, :]
    gain[...] = small[EXPERTS : EXPERTS + 1, :]
    for load, store in zip(loads, stores):
        load.wait()
        store.start()
    for cp in stores:
        cp.wait()


def finish(arrays):
    vmem = pl.BlockSpec(memory_space=pltpu.VMEM)
    hbm = pl.BlockSpec(memory_space=pl.ANY)
    return pl.pallas_call(
        finish_kernel,
        out_shape=tuple(jax.ShapeDtypeStruct(a.shape, a.dtype) for a in arrays[:5])
        + (jax.ShapeDtypeStruct((EXPERTS, QB), F32), jax.ShapeDtypeStruct((1, QB), F32)),
        in_specs=[hbm] * 5 + [vmem],
        out_specs=(hbm,) * 5 + (vmem, vmem),
        scratch_shapes=[pltpu.VMEM(a.shape, a.dtype) for a in arrays[:5]]
        + [pltpu.SemaphoreType.DMA((2, 5))],
        compiler_params=pltpu.CompilerParams(vmem_limit_bytes=62 * 1024 * 1024),
        cost_estimate=pl.CostEstimate(flops=0, bytes_accessed=20_000_000, transcendentals=0),
    )(*arrays)


def on_device(
    incoming, hidden, expert_out, routes, expert_back, scan_out, gate_in, w_out, w_router, norm_gain
):
    outs = layer(
        incoming[0], hidden[0], expert_out[0], jnp.swapaxes(routes[0], 1, 2), expert_back[0],
        scan_out[0], gate_in[0], w_out[0], w_router[0].T, norm_gain,
    )
    passed, scan_grad, gate_grad, expert_grad, weight_grad, router, gain = finish(outs)
    return (
        passed[None],
        scan_grad[None],
        gate_grad[None],
        expert_grad[None],
        weight_grad[None],
        router.T[None],
        gain,
    )


def solution(mesh):
    placed = (
        P("section", None, ("dp", "tensor"), None),
        P("section", None, ("dp", "tensor"), None),
        P("section", None, ("dp", "tensor"), None, None),
        P("section", None, ("dp", "tensor"), None),
        P("section", None, ("dp", "tensor"), None),
        P("section", None, "dp", "tensor"),
        P("section", None, "dp", "tensor"),
        P("section", "tensor", None),
        P("section", "dp", None),
        P("section", "dp"),
    )
    return jax.shard_map(
        on_device,
        mesh=mesh,
        in_specs=placed,
        out_specs=(
            P("section", None, ("dp", "tensor"), None),
            P("section", None, "dp", "tensor"),
            P("section", None, "dp", "tensor"),
            P("section", None, ("dp", "tensor"), None),
            P("section", "tensor", "dp"),
            P("section", "dp", None),
            P("section", "dp"),
        ),
        check_vma=False,
    )
```
